32 devices in a mesh: dp: 8 (over y, x, core), tensor: 4 (over z).
Axes of the slice: x: 2, y: 2, z: 4, core: 2. Of those that a mesh axis runs over, the one named last changes fastest.
Arguments:
- tokens: bfloat16 [8192, 2048], P(('dp', 'tensor')), may hold values from -6 to 6
- cotangent: bfloat16 [8192, 2048], P(('dp', 'tensor')), may hold values from -6 to 6
- norm_gains: float32 [2, 2048], replicated, may hold values from 0.1 to 1.9
- norm_shifts: float32 [2, 2048], replicated, may hold values from -4 to 4
- query_key_value_weight: bfloat16 [2048, 3, 2048], P(None, None, 'tensor'), may hold values from -0.125 to 0.125
- b_qv: float32 [2, 2048], P(None, 'tensor'), may hold values from -4 to 4
- output_weight: bfloat16 [2048, 2048], P('tensor'), may hold values from -0.375 to 0.375
- output_bias_vector: float32 [2048], replicated, may hold values from -4 to 4
- up_weight: bfloat16 [2048, 8192], P(None, 'tensor'), may hold values from -0.125 to 0.125
- b_up: float32 [8192], P('tensor'), may hold values from -4 to 4
- down_weight: bfloat16 [8192, 2048], P('tensor'), may hold values from -0.0625 to 0.0625
- down_bias_vector: float32 [2048], replicated, may hold values from -4 to 4
- adapter_query_key_value_input: bfloat16 [8, 16, 2048], replicated, may hold values from -0.125 to 0.125
- qkv_out: bfloat16 [8, 16, 3, 2048], P(None, None, None, 'tensor'), may hold values from -1.5 to 1.5
- adapter_output_input: bfloat16 [8, 16, 2048], P(None, None, 'tensor'), may hold values from -0.375 to 0.375
- adapter_output_output: bfloat16 [8, 16, 2048], replicated, may hold values from -1.5 to 1.5
- adapter_up_input: bfloat16 [8, 16, 2048], replicated, may hold values from -0.125 to 0.125
- up_out: bfloat16 [8, 16, 8192], P(None, None, 'tensor'), may hold values from -1.5 to 1.5
- down_in: bfloat16 [8, 16, 8192], P(None, None, 'tensor'), may hold values from -0.0625 to 0.0625
- adapter_down_output: bfloat16 [8, 16, 2048], replicated, may hold values from -1.5 to 1.5
- offsets: int32 [8, 2], P('dp'), may hold values from 0 to 768, as said below
- adapter_ids: int32 [8, 4], P('dp'), may hold values from 0 to 7
Outputs:
- out: bfloat16 [8192, 2048], P(('dp', 'tensor'))
- in_grad: bfloat16 [8192, 2048], P(('dp', 'tensor'))
- g_qkv_in: float32 [8, 16, 2048], replicated
- g_qkv_out: float32 [8, 16, 3, 2048], P(None, None, None, 'tensor')
- g_out_in: float32 [8, 16, 2048], P(None, None, 'tensor')
- g_out_out: float32 [8, 16, 2048], replicated
- g_up_in: float32 [8, 16, 2048], replicated
- g_up_out: float32 [8, 16, 8192], P(None, None, 'tensor')
- g_down_in: float32 [8, 16, 8192], P(None, None, 'tensor')
- g_down_out: float32 [8, 16, 2048], replicated
The draws below stay inside these ranges and needn't reach their ends.
Inputs may be any that keep to these rules, and one draw needn't show every extreme that they name: For every sequence s, offsets[s, 0] + 256 <= offsets[s, 1]: the two pieces of 256 positions lie inside the sequence and don't intersect.
All inputs are finite; a program needn't handle non-finite values.
Results may differ from the reference program's by a relative error of at most 0.02.
Values may be sent and summed in bfloat16 or wider, within the bound.
A program may use at most 192 MiB of HBM per device.

```python
import math
import jax
import jax.numpy as jnp
from jax import lax

D = 2048
HEADS = 16
HEAD_DIM = 128
FF = 8192
RANK = 16
ADAPTERS = 8
LEN = 1024
PIECE = 256
SEQS = 8
TOKENS = 8192


def draw_offsets(key, part):
    subkeys = jax.random.split(key, 4)
    first_start = jax.random.randint(subkeys[0], (SEQS,), 0, LEN - 2 * PIECE + 1)
    second_start = jax.random.randint(subkeys[1], (SEQS,), first_start + PIECE, LEN - PIECE + 1)
    seq_index = jnp.arange(SEQS)
    high_row = jax.random.randint(subkeys[2], (), 0, SEQS)
    low_row = jax.random.randint(subkeys[3], (), 0, SEQS)
    second_start = jnp.where(seq_index == high_row, LEN - PIECE, second_start)
    first_start = jnp.where(seq_index == low_row, 0, first_start)
    return jnp.stack([first_start, second_start], axis=1).astype(jnp.int32)


def touch_ends(array, key, low, largest):
    longest = array.shape.index(max(array.shape))
    spots = []
    for shift in (0, 1):
        where = [jax.random.randint(jax.random.fold_in(key, axis), (), 0, length) for axis, length in enumerate(array.shape)]
        where[longest] = (where[longest] + shift) % array.shape[longest]
        spots.append(tuple(where))
    return array.at[spots[0]].set(low).at[spots[1]].set(largest)


def steps_of(rng, shape, cuts, low, largest):
    gain, own = 1.0, jax.random.fold_in(rng, 6)
    for dim, blocks in cuts:
        steps = jnp.exp(jax.random.uniform(jax.random.fold_in(own, dim), (blocks,), jnp.float32, low / len(cuts), largest / len(cuts)))
        gain = gain * jnp.repeat(steps, shape[dim] // blocks).reshape([-1 if axis == dim else 1 for axis in range(len(shape))])
    return gain


def scatter_about(rng, extent, deviation, limit, cuts=(), held_as=jnp.bfloat16):
    values = jax.random.normal(rng, extent, jnp.float32) * deviation
    if len(cuts) > 0:
        values = steps_of(rng, extent, cuts, -0.22, 0.18) * values
    return jnp.clip(values, min=-limit, max=limit).astype(held_as)


def setup_inputs(seed: int = 0) -> dict:
    seeds = jax.random.split(jax.random.key(seed), 23)
    tokens = scatter_about(seeds[0], (TOKENS, D), 1.0, 6.0, ((0, 32),))
    cotangent = scatter_about(seeds[1], (TOKENS, D), 1.0, 6.0, ((0, 32),))
    norm_gains = jnp.clip(1.0 + 0.18 * jax.random.normal(seeds[2], (2, D), jnp.float32), 0.1, 1.9)
    norm_shifts = scatter_about(seeds[3], (2, D), 0.3, 4.0, (), jnp.float32)
    query_key_value_weight = scatter_about(seeds[4], (D, 3, D), D ** -0.5, 0.125, ((2, 4),))
    b_qv = scatter_about(seeds[5], (2, D), 0.3, 4.0, ((1, 4),), jnp.float32)
    output_weight = scatter_about(seeds[6], (D, D), (D // 8) ** -0.5, 0.375, ((0, 4),))
    output_bias_vector = scatter_about(seeds[7], (D,), 0.3, 4.0, (), jnp.float32)
    up_weight = scatter_about(seeds[8], (D, FF), D ** -0.5, 0.125, ((1, 4),))
    b_up = scatter_about(seeds[9], (FF,), 0.3, 4.0, ((0, 4),), jnp.float32)
    down_weight = scatter_about(seeds[10], (FF, D), FF ** -0.5, 0.0625, ((0, 4),))
    down_bias_vector = scatter_about(seeds[11], (D,), 0.3, 4.0, (), jnp.float32)
    adapter_query_key_value_input = scatter_about(seeds[12], (ADAPTERS, RANK, D), D ** -0.5, 0.125)
    qkv_out = scatter_about(seeds[13], (ADAPTERS, RANK, 3, D), RANK ** -0.5, 1.5, ((3, 4),))
    adapter_output_input = scatter_about(seeds[14], (ADAPTERS, RANK, D), (D // 8) ** -0.5, 0.375, ((2, 4),))
    adapter_output_output = scatter_about(seeds[15], (ADAPTERS, RANK, D), RANK ** -0.5, 1.5)
    adapter_up_input = scatter_about(seeds[16], (ADAPTERS, RANK, D), D ** -0.5, 0.125)
    up_out = scatter_about(seeds[17], (ADAPTERS, RANK, FF), RANK ** -0.5, 1.5, ((2, 4),))
    down_in = scatter_about(seeds[18], (ADAPTERS, RANK, FF), FF ** -0.5, 0.0625, ((2, 4),))
    adapter_down_output = scatter_about(seeds[19], (ADAPTERS, RANK, D), RANK ** -0.5, 1.5)
    offsets = draw_offsets(jax.random.fold_in(seeds[22], 71), 0)
    adapter_ids = touch_ends(jax.random.randint(seeds[21], (SEQS, 4), 0, ADAPTERS), jax.random.fold_in(seeds[21], 1), 0, ADAPTERS - 1).astype(jnp.int32)
    return dict(tokens=tokens, cotangent=cotangent, norm_gains=norm_gains, norm_shifts=norm_shifts, query_key_value_weight=query_key_value_weight, b_qv=b_qv, output_weight=output_weight, output_bias_vector=output_bias_vector, up_weight=up_weight, b_up=b_up, down_weight=down_weight, down_bias_vector=down_bias_vector, adapter_query_key_value_input=adapter_query_key_value_input, qkv_out=qkv_out, adapter_output_input=adapter_output_input, adapter_output_output=adapter_output_output, adapter_up_input=adapter_up_input, up_out=up_out, down_in=down_in, adapter_down_output=adapter_down_output, offsets=offsets, adapter_ids=adapter_ids)


EPS = 1e-05
GELU_C = 0.7978845608028654
GELU_K = 0.044715
NEGATIVE = -1e+30
EXACT_MODE = lax.Precision.HIGHEST

@jax.custom_vjp
def low(v):
    return lax.optimization_barrier(v.astype(jnp.bfloat16)).astype(jnp.float32)

@jax.custom_vjp
def low_back(v):
    return v

def low_keep(v):
    return (low(v), None)

def low_pass(kept, grad):
    return (grad,)

def back_keep(v):
    return (v, None)

def back_low(kept, grad):
    return (low(grad),)
low.defvjp(low_keep, low_pass)
low_back.defvjp(back_keep, back_low)

def gelu_tanh(values):
    return 0.5 * values * (1.0 + jnp.tanh(GELU_C * (values + GELU_K * values * values * values)))

def layer_norm(values, gain_row, shift_row):
    centre = values - lax.optimization_barrier(jnp.mean(values, axis=-1, keepdims=True))
    spread = lax.optimization_barrier(jnp.mean(centre * centre, axis=-1, keepdims=True))
    return centre * lax.rsqrt(spread + EPS) * gain_row + shift_row

def select_adapter_maps(adapter_table, indicator_matrix):
    return jnp.einsum('se,e...->s...', indicator_matrix, adapter_table, precision=EXACT_MODE)

def piece_ids(offsets):
    where_at = jnp.arange(LEN).astype(jnp.int32)
    first_piece = ((where_at[None, :] >= offsets[:, 0:1]) & (where_at[None, :] < offsets[:, 0:1] + PIECE)).astype(jnp.int32)
    second_piece = ((where_at[None, :] >= offsets[:, 1:2]) & (where_at[None, :] < offsets[:, 1:2] + PIECE)).astype(jnp.int32)
    return first_piece + 2 * second_piece

def attention(queries, keys_all, values, pieces):
    block_rows = min(512, LEN)
    block_count = LEN // block_rows
    slopes = jnp.exp2(-8.0 * (jnp.arange(HEADS).astype(jnp.float32) + 1.0) / HEADS)
    keys_at = jnp.arange(LEN).astype(jnp.int32)
    scaling = 1.0 / math.sqrt(HEAD_DIM)

    def query_block(block_index):
        first_row = (block_index * block_rows).astype(jnp.int32)
        query_rows = lax.dynamic_slice_in_dim(queries, first_row, block_rows, 1)
        query_at = first_row + jnp.arange(block_rows).astype(jnp.int32)
        piece_rows = lax.dynamic_slice_in_dim(pieces, first_row, block_rows, 1)
        scores = jnp.einsum('sqhd,skhd->shqk', query_rows, keys_all, precision=EXACT_MODE) * scaling
        distance = jnp.abs(query_at[:, None] - keys_at[None, :]).astype(jnp.float32)
        scores = scores - slopes[None, :, None, None] * distance[None, None]
        allowed = (keys_at[None, None, :] <= query_at[None, :, None]) | (piece_rows[:, :, None] == pieces[:, None, :]) & (piece_rows[:, :, None] > 0)
        scores = jnp.where(allowed[:, None], scores, NEGATIVE)
        scores = low_back(scores)
        weights = low(jax.nn.softmax(scores, axis=-1))
        return jnp.einsum('shqk,skhd->sqhd', weights, values, precision=EXACT_MODE)
    blocks = lax.map(jax.checkpoint(query_block), jnp.arange(block_count).astype(jnp.int32))
    return jnp.moveaxis(blocks, 0, 1).reshape(queries.shape)

def layer(tokens, adapters, frozen, pieces, indicator_matrix):
    adapter_query_key_value_input, qkv_out, adapter_output_input, adapter_output_output, adapter_up_input, up_out, down_in, adapter_down_output = adapters
    norm_gains, norm_shifts, query_key_value_weight, b_qv, output_weight, output_bias_vector, up_weight, b_up, down_weight, down_bias_vector = frozen
    seq_here = tokens.shape[0]
    normalized_input = low(layer_norm(tokens, norm_gains[0], norm_shifts[0]))
    low_rank_query_key_value = jnp.einsum('utc,ugc->utg', normalized_input, select_adapter_maps(adapter_query_key_value_input, indicator_matrix[:, 0]), precision=EXACT_MODE)
    projection_result = jnp.einsum('kyz,zfq->kyfq', normalized_input, query_key_value_weight, precision=EXACT_MODE)
    projection_result = projection_result + jnp.einsum('slr,srcm->slcm', low_rank_query_key_value, select_adapter_maps(qkv_out, indicator_matrix[:, 0]), precision=EXACT_MODE)
    qkv_bias = jnp.stack([b_qv[0], jnp.zeros_like(b_qv[0]), b_qv[1]], 0)
    projection_result = projection_result + qkv_bias
    head_shape = (seq_here, LEN, HEADS, HEAD_DIM)
    queries = low(low_back(projection_result[:, :, 0])).reshape(head_shape)
    keys_all = low(low_back(projection_result[:, :, 1])).reshape(head_shape)
    values = low(low_back(projection_result[:, :, 2])).reshape(head_shape)
    attended_context = attention(queries, keys_all, values, pieces)
    attended_context = low(low_back(attended_context.reshape(seq_here, LEN, D)))
    low_rank_output = jnp.einsum('utc,ugc->utg', attended_context, select_adapter_maps(adapter_output_input, indicator_matrix[:, 1]), precision=EXACT_MODE)
    side_path = jnp.einsum('rzv,vu->rzu', attended_context, output_weight, precision=EXACT_MODE)
    side_path = side_path + jnp.einsum('unz,uzh->unh', low_rank_output, select_adapter_maps(adapter_output_output, indicator_matrix[:, 1]), precision=EXACT_MODE) + output_bias_vector
    middle = tokens + low_back(side_path)
    normalized_middle = low(layer_norm(middle, norm_gains[1], norm_shifts[1]))
    low_rank_upward = jnp.einsum('utc,ugc->utg', normalized_middle, select_adapter_maps(adapter_up_input, indicator_matrix[:, 2]), precision=EXACT_MODE)
    gate_input_rows = jnp.einsum('zme,en->zmn', normalized_middle, up_weight, precision=EXACT_MODE)
    gate_input_rows = gate_input_rows + jnp.einsum('slr,srf->slf', low_rank_upward, select_adapter_maps(up_out, indicator_matrix[:, 2]), precision=EXACT_MODE) + b_up
    hidden_rows = low(gelu_tanh(low_back(gate_input_rows)))
    low_rank_down = jnp.einsum('slf,srf->slr', hidden_rows, select_adapter_maps(down_in, indicator_matrix[:, 3]), precision=EXACT_MODE)
    feedforward_path = jnp.einsum('qni,ij->qnj', hidden_rows, down_weight, precision=EXACT_MODE)
    feedforward_path = feedforward_path + jnp.einsum('unz,uzh->unh', low_rank_down, select_adapter_maps(adapter_down_output, indicator_matrix[:, 3]), precision=EXACT_MODE) + down_bias_vector
    return middle + feedforward_path

def reference(tokens, cotangent, norm_gains, norm_shifts, query_key_value_weight, b_qv, output_weight, output_bias_vector, up_weight, b_up, down_weight, down_bias_vector, adapter_query_key_value_input, qkv_out, adapter_output_input, adapter_output_output, adapter_up_input, up_out, down_in, adapter_down_output, offsets, adapter_ids):
    seq_group = 4
    step_total = SEQS // seq_group
    frozen = tuple((member.astype(jnp.float32) for member in (norm_gains, norm_shifts, query_key_value_weight, b_qv, output_weight, output_bias_vector, up_weight, b_up, down_weight, down_bias_vector)))
    adapters = tuple((member.astype(jnp.float32) for member in (adapter_query_key_value_input, qkv_out, adapter_output_input, adapter_output_output, adapter_up_input, up_out, down_in, adapter_down_output)))
    inputs = tokens.astype(jnp.float32).reshape(step_total, seq_group, LEN, D)
    grads_in = cotangent.astype(jnp.float32).reshape(step_total, seq_group, LEN, D)
    pieces = piece_ids(offsets).reshape(step_total, seq_group, LEN)
    table_ids = jnp.arange(ADAPTERS).astype(jnp.int32)
    indicator_matrix = (adapter_ids[:, :, None] == table_ids[None, None, :]).astype(jnp.float32)
    indicator_matrix = indicator_matrix.reshape(step_total, seq_group, 4, ADAPTERS)

    def one_step(totals, step_items):
        inputs_here, grads_here, pieces_here, hot_here = step_items

        def forward(values, tables):
            return layer(values, tables, frozen, pieces_here, hot_here)
        result, pullback = jax.vjp(forward, inputs_here, adapters)
        grad_values, grad_tables = pullback(grads_here)
        totals = tuple((running + addition for running, addition in zip(totals, grad_tables)))
        return (totals, (result.astype(jnp.bfloat16), grad_values.astype(jnp.bfloat16)))
    zero_tables = tuple((jnp.zeros(member.shape, jnp.float32) for member in adapters))
    totals, (outputs, grads_out) = lax.scan(one_step, zero_tables, (inputs, grads_in, pieces, indicator_matrix))
    return (outputs.reshape(TOKENS, D), grads_out.reshape(TOKENS, D), totals[0], totals[1], totals[2], totals[3], totals[4], totals[5], totals[6], totals[7])
```

```python
import functools
import math

import jax
import jax.numpy as jnp
from jax import lax
from jax.experimental import pallas as pl
from jax.experimental.pallas import tpu as pltpu
from jax.sharding import PartitionSpec as P

HEADS = 16
HEAD_DIM = 128
PIECE = 256
PAD = 128
EPS = 1e-05
GELU_C = 0.7978845608028654
GELU_K = 0.044715
LOG2E = 1.4426950408889634
FAR = 1e32
F32 = jnp.float32
BF16 = jnp.bfloat16
AXES = ("dp", "tensor")
SLOT = (0, 2, 1, 3)
VM = pltpu.VMEM


def dot(a, b):
    return lax.dot_general(a, b, (((1,), (0,)), ((), ())), preferred_element_type=F32)


def dot_t(a, b):
    return lax.dot_general(a, b, (((1,), (1,)), ((), ())), preferred_element_type=F32)


def t_dot(a, b):
    return lax.dot_general(a, b, (((0,), (0,)), ((), ())), preferred_element_type=F32)


def whole(shape):
    zeros = (0,) * len(shape)
    return pl.BlockSpec(shape, lambda *_: zeros)


def params(mib=56):
    return pltpu.CompilerParams(vmem_limit_bytes=mib << 20)


def cost(flops, read):
    return pl.CostEstimate(flops=int(flops), bytes_accessed=int(read), transcendentals=0)


def fwd_qkv_kernel(x, w, a, b, bias, out, rank):
    @pl.when(pl.program_id(0) == 0)
    def _():
        rank[...] = dot_t(x[...], a[...]).astype(BF16)

    out[...] = (dot(x[...], w[0]) + dot(rank[...], b[...]) + bias[...]).astype(BF16)


def fwd_qkv(x, w3, a, b, bias):
    n, k = x.shape
    cols = w3.shape[2]
    return pl.pallas_call(
        fwd_qkv_kernel,
        grid=(3,),
        in_specs=[
            whole((n, k)),
            pl.BlockSpec((1, k, cols), lambda j: (j, 0, 0)),
            whole(a.shape),
            pl.BlockSpec((PAD, cols), lambda j: (0, j)),
            pl.BlockSpec((1, cols), lambda j: (0, j)),
        ],
        out_specs=[pl.BlockSpec((n, cols), lambda j: (0, j)), whole((n, PAD))],
        out_shape=[jax.ShapeDtypeStruct((n, 3 * cols), BF16), jax.ShapeDtypeStruct((n, PAD), BF16)],
        compiler_params=params(),
        cost_estimate=cost(6 * n * k * cols, 2 * (n * k + 3 * k * cols)),
        name="fwd_qkv",
    )(x, w3, a, b, bias)


def fwd_o_kernel(x, w, a, b, out, rank):
    r = dot_t(x[...], a[...]).astype(BF16)
    rank[...] = r
    out[...] = (dot(x[...], w[...]) + dot(r, b[...])).astype(BF16)


def fwd_o(x, w, a, b, tile):
    n, k = x.shape
    cols = w.shape[1]
    return pl.pallas_call(
        fwd_o_kernel,
        grid=(n // tile,),
        in_specs=[pl.BlockSpec((tile, k), lambda i: (i, 0)), whole(w.shape), whole(a.shape), whole(b.shape)],
        out_specs=[pl.BlockSpec((tile, cols), lambda i: (i, 0)), pl.BlockSpec((tile, PAD), lambda i: (i, 0))],
        out_shape=[jax.ShapeDtypeStruct((n, cols), BF16), jax.ShapeDtypeStruct((n, PAD), BF16)],
        compiler_params=params(),
        cost_estimate=cost(2 * n * k * cols, 2 * (n * k + k * cols + n * cols)),
        name="fwd_o",
    )(x, w, a, b)


def bwd_o_kernel(g, w, b, a, rank, x, out, tb, ta):
    first = pl.program_id(0) == 0
    r = dot_t(g[...], b[...]).astype(BF16)
    out[...] = (dot_t(g[...], w[...]) + dot(r, a[...])).astype(BF16)
    one = t_dot(rank[...], g[...])
    two = t_dot(r, x[...])

    @pl.when(first)
    def _():
        tb[...] = one
        ta[...] = two

    @pl.when(jnp.logical_not(first))
    def _():
        tb[...] += one
        ta[...] += two


def bwd_o(g, w, b, a, rank, x, tile):
    n, k = g.shape
    cols = w.shape[0]
    row = lambda c: pl.BlockSpec((tile, c), lambda i: (i, 0))
    return pl.pallas_call(
        bwd_o_kernel,
        grid=(n // tile,),
        in_specs=[row(k), whole(w.shape), whole(b.shape), whole(a.shape), row(PAD), row(cols)],
        out_specs=[row(cols), whole((PAD, k)), whole((PAD, cols))],
        out_shape=[
            jax.ShapeDtypeStruct((n, cols), BF16),
            jax.ShapeDtypeStruct((PAD, k), F32),
            jax.ShapeDtypeStruct((PAD, cols), F32),
        ],
        compiler_params=params(),
        cost_estimate=cost(2 * n * k * cols, 2 * (n * k + k * cols + n * cols)),
        name="bwd_o",
    )(g, w, b, a, rank, x)


def bwd_qkv_kernel(g, w, b, a, rank, x, out, tb, ta):
    first = pl.program_id(0) == 0
    cols = w.shape[2]
    r = dot_t(g[...], b[...]).astype(BF16)
    acc = dot(r, a[...])
    for j in range(3):
        acc = acc + dot_t(g[:, j * cols : (j + 1) * cols], w[j])
    out[...] = acc.astype(BF16)
    one = t_dot(rank[...], g[...])
    two = t_dot(r, x[...])

    @pl.when(first)
    def _():
        tb[...] = one
        ta[...] = two

    @pl.when(jnp.logical_not(first))
    def _():
        tb[...] += one
        ta[...] += two


def bwd_qkv(g, w3, b, a, rank, x, tile):
    n, k = g.shape
    cols = w3.shape[1]
    row = lambda c: pl.BlockSpec((tile, c), lambda i: (i, 0))
    return pl.pallas_call(
        bwd_qkv_kernel,
        grid=(n // tile,),
        in_specs=[row(k), whole(w3.shape), whole(b.shape), whole(a.shape), row(PAD), row(cols)],
        out_specs=[row(cols), whole((PAD, k)), whole((PAD, cols))],
        out_shape=[
            jax.ShapeDtypeStruct((n, cols), BF16),
            jax.ShapeDtypeStruct((PAD, k), F32),
            jax.ShapeDtypeStruct((PAD, cols), F32),
        ],
        compiler_params=params(),
        cost_estimate=cost(2 * n * k * cols, 2 * (n * k + k * cols + n * cols)),
        name="bwd_qkv",
    )(g, w3, b, a, rank, x)


def distances(ints, rows, step, dist):
    me, s0, s1 = ints[0], ints[1], ints[2]
    length = dist.shape[0]

    def piece(pos, none):
        one = jnp.where((pos >= s0) & (pos < s0 + PIECE), 1, none)
        return jnp.where((pos >= s1) & (pos < s1 + PIECE), 2, one)

    def rel(j):
        return ((j & 1) << 1) | (j >> 1)

    i = lax.broadcasted_iota(jnp.int32, (length, PAD), 0)
    kpos = (me ^ rel(i // rows)) * rows + i % rows
    kpos = kpos[:, :1]
    qpos = (me ^ rel(step)) * rows + lax.broadcasted_iota(jnp.int32, (1, rows), 1)
    seen = (kpos <= qpos) | (piece(kpos, -1) == piece(qpos, -2))
    dist[...] = jnp.where(seen, jnp.abs(kpos - qpos).astype(F32), FAR)


def attend_kernel(ints, slopes, q, k, v, ctx, lse, dist, vt):
    step = pl.program_id(0)
    rows = q.shape[0]
    heads = q.shape[1] // HEAD_DIM
    scale = LOG2E / math.sqrt(HEAD_DIM)
    distances(ints, rows, step, dist)

    @pl.when(step == 0)
    def _():
        vt[...] = v[...].T

    for h in range(heads):
        span = slice(h * HEAD_DIM, (h + 1) * HEAD_DIM)
        s = dot_t(k[:, span], q[:, span]) * scale - dist[...] * (slopes[h] * LOG2E)
        peak = jnp.max(s, axis=0, keepdims=True)
        e = jnp.exp2(s - peak)
        total = jnp.sum(e, axis=0, keepdims=True)
        c = dot(vt[span, :], e.astype(BF16)) * (1.0 / total)
        ctx[:, span] = c.T.astype(BF16)
        lse[h : h + 1, :] = peak + jnp.log2(total)


def attend(ints, slopes, proj, rows):
    length, three = proj.shape
    local = three // 3
    heads = local // HEAD_DIM
    return pl.pallas_call(
        attend_kernel,
        grid_spec=pltpu.PrefetchScalarGridSpec(
            num_scalar_prefetch=2,
            grid=(length // rows,),
            in_specs=[
                pl.BlockSpec((rows, local), lambda i, *_: (i, 0)),
                pl.BlockSpec((length, local), lambda i, *_: (0, 1)),
                pl.BlockSpec((length, local), lambda i, *_: (0, 2)),
            ],
            out_specs=[
                pl.BlockSpec((rows, local), lambda i, *_: (i, 0)),
                pl.BlockSpec((heads, rows), lambda i, *_: (0, i)),
            ],
            scratch_shapes=[VM((length, rows), F32), VM((local, length), BF16)],
        ),
        out_shape=[jax.ShapeDtypeStruct((length, local), BF16), jax.ShapeDtypeStruct((heads, length), F32)],
        compiler_params=params(),
        cost_estimate=cost(4 * length * length * local, 8 * length * local),
        name="attend",
    )(ints, slopes, proj, proj, proj)


def attend_back_kernel(ints, slopes, q, k, v, g, lse, out, dist, kt, gk, gv):
    step = pl.program_id(0)
    rows = q.shape[0]
    local = q.shape[1]
    heads = local // HEAD_DIM
    scale = 1.0 / math.sqrt(HEAD_DIM)
    distances(ints, rows, step, dist)

    @pl.when(step == 0)
    def _():
        kt[...] = k[...].T
        gk[...] = jnp.zeros_like(gk)
        gv[...] = jnp.zeros_like(gv)

    at = pl.ds(pl.multiple_of(step * rows, rows), rows)
    for h in range(heads):
        span = slice(h * HEAD_DIM, (h + 1) * HEAD_DIM)
        s = dot_t(k[:, span], q[:, span]) * (scale * LOG2E) - dist[...] * (slopes[h] * LOG2E)
        p = jnp.exp2(s - lse[h : h + 1, :])
        gv[:, span] += dot(p.astype(BF16), g[:, span])
        gp = dot_t(v[:, span], g[:, span])
        inner = jnp.sum(p * gp, axis=0, keepdims=True)
        gs = (p * (gp - inner)).astype(BF16)
        gk[:, span] += dot(gs, q[:, span])
        out[at, span] = (dot(kt[span, :], gs).T * scale).astype(BF16)

    @pl.when(step == pl.num_programs(0) - 1)
    def _():
        out[:, local : 2 * local] = (gk[...] * scale).astype(BF16)
        out[:, 2 * local :] = gv[...].astype(BF16)


def attend_back(ints, slopes, proj, g, lse, rows):
    length, three = proj.shape
    local = three // 3
    heads = local // HEAD_DIM
    return pl.pallas_call(
        attend_back_kernel,
        grid_spec=pltpu.PrefetchScalarGridSpec(
            num_scalar_prefetch=2,
            grid=(length // rows,),
            in_specs=[
                pl.BlockSpec((rows, local), lambda i, *_: (i, 0)),
                pl.BlockSpec((length, local), lambda i, *_: (0, 1)),
                pl.BlockSpec((length, local), lambda i, *_: (0, 2)),
                pl.BlockSpec((rows, local), lambda i, *_: (i, 0)),
                pl.BlockSpec((heads, rows), lambda i, *_: (0, i)),
            ],
            out_specs=pl.BlockSpec((length, three), lambda i, *_: (0, 0)),
            scratch_shapes=[
                VM((length, rows), F32),
                VM((local, length), BF16),
                VM((length, local), F32),
                VM((length, local), F32),
            ],
        ),
        out_shape=jax.ShapeDtypeStruct((length, three), BF16),
        compiler_params=params(),
        cost_estimate=cost(10 * length * length * local, 16 * length * local),
        name="attend_back",
    )(ints, slopes, proj, proj, proj, g, lse)


def gelu_parts(values):
    square = values * values
    tangent = jnp.tanh(GELU_C * (values + GELU_K * square * values))
    half = 0.5 * (1.0 + tangent)
    slope = half + (0.5 * GELU_C) * values * (1.0 - tangent * tangent) * (1.0 + 3.0 * GELU_K * square)
    return values * half, slope


def mlp_kernel(
    n0, n1, c0, c1, wu, wd, au, bu, ad, bd, bias, part, back, tuo, tdi, tui, tdo,
    nm, cot, up_rank, down_rank, g_up, g_down, acc, gacc,
):
    step = pl.program_id(0)
    last = pl.num_programs(0) - 1
    rows = n0.shape[0]

    @pl.when(step == 0)
    def _():
        nm[:rows] = n0[...]
        nm[rows:] = n1[...]
        cot[:rows] = c0[...]
        cot[rows:] = c1[...]
        up_rank[...] = dot_t(nm[...], au[...]).astype(BF16)
        g_down[...] = dot_t(cot[...], bd[...]).astype(BF16)
        down_rank[...] = jnp.zeros_like(down_rank)
        g_up[...] = jnp.zeros_like(g_up)
        acc[...] = jnp.zeros_like(acc)
        gacc[...] = jnp.zeros_like(gacc)

    gate = dot(nm[...], wu[...]) + dot(up_rank[...], bu[...]) + bias[...]
    value, slope = gelu_parts(gate)
    hidden = value.astype(BF16)
    grad = dot_t(cot[...], wd[...]) + dot(g_down[...], ad[...])
    grad_gate = (grad * slope).astype(BF16)
    down_rank[...] += dot_t(hidden, ad[...])
    g_up[...] += dot_t(grad_gate, bu[...])
    acc[...] += dot(hidden, wd[...])
    gacc[...] += dot_t(grad_gate, wu[...])
    tuo[...] = t_dot(up_rank[...], grad_gate)
    tdi[...] = t_dot(g_down[...], hidden)

    @pl.when(step == last)
    def _():
        dr = down_rank[...].astype(BF16)
        gu = g_up[...].astype(BF16)
        part[...] = (acc[...] + dot(dr, bd[...])).astype(BF16)
        back[...] = (gacc[...] + dot(gu, au[...])).astype(BF16)
        tui[...] = t_dot(gu, nm[...])
        tdo[...] = t_dot(dr, cot[...])


def mlp(n0, n1, c0, c1, wu, wd, au, bu, ad, bd, bias, tile):
    rows, width = n0.shape
    n = 2 * rows
    hidden = wu.shape[1]
    cut = lambda r: pl.BlockSpec((r, tile), lambda j: (0, j))
    return pl.pallas_call(
        mlp_kernel,
        grid=(hidden // tile,),
        in_specs=[
            whole((rows, width)), whole((rows, width)), whole((rows, width)), whole((rows, width)),
            cut(width), pl.BlockSpec((tile, width), lambda j: (j, 0)),
            whole(au.shape), cut(PAD), cut(PAD), whole(bd.shape), cut(1),
        ],
        out_specs=[
            whole((n, width)), whole((n, width)), cut(PAD), cut(PAD), whole((PAD, width)), whole((PAD, width)),
        ],
        out_shape=[
            jax.ShapeDtypeStruct((n, width), BF16),
            jax.ShapeDtypeStruct((n, width), BF16),
            jax.ShapeDtypeStruct((PAD, hidden), F32),
            jax.ShapeDtypeStruct((PAD, hidden), F32),
            jax.ShapeDtypeStruct((PAD, width), F32),
            jax.ShapeDtypeStruct((PAD, width), F32),
        ],
        scratch_shapes=[
            VM((n, width), BF16), VM((n, width), BF16), VM((n, PAD), BF16), VM((n, PAD), F32), VM((n, PAD), F32),
            VM((n, PAD), BF16), VM((n, width), F32), VM((n, width), F32),
        ],
        compiler_params=params(60),
        cost_estimate=cost(8 * n * width * hidden, 4 * width * hidden + 12 * n * width),
        name="mlp",
    )(n0, n1, c0, c1, wu, wd, au, bu, ad, bd, bias)


MESH = pl.DeviceIdType.MESH
CHUNKS = 4


def places():
    d, t = lax.axis_index("dp"), lax.axis_index("tensor")
    core, zh = d % 2, t // 2
    core_d = d + 1 - 2 * core
    near_t = t + 1 - 2 * (t % 2)
    left = d + 2 - 4 * ((d // 2) % 2)
    up = 4 - 8 * ((d // 4) % 2)
    return dict(
        moved=(core + zh) % 2 == 1,
        line=(d // 2) % 4,
        core=(core_d, t),
        near=(d, near_t),
        cross=(core_d, t + 2 - 4 * zh),
        left=(left, t),
        up=(d + up, t),
        both=(left + up, t),
    )


def greet(always, sometimes=(), when=None):
    barrier = pltpu.get_barrier_semaphore()
    for peer in always:
        pl.semaphore_signal(barrier, inc=1, device_id=peer, device_id_type=MESH)
    count = len(always)
    if sometimes:

        @pl.when(when)
        def _():
            for peer in sometimes:
                pl.semaphore_signal(barrier, inc=1, device_id=peer, device_id_type=MESH)

        count = count + len(sometimes) * when.astype(jnp.int32)
    pl.semaphore_wait(barrier, count)


def remote(src, dst, send, recv, peer):
    return pltpu.make_async_remote_copy(
        src_ref=src, dst_ref=dst, send_sem=send, recv_sem=recv, device_id=peer, device_id_type=MESH
    )


def unit_rows(v):
    centre = v - jnp.mean(v, axis=-1, keepdims=True)
    inverse = lax.rsqrt(jnp.mean(centre * centre, axis=-1, keepdims=True) + EPS)
    return centre * inverse, inverse


def unit_back(grad, scaled, inverse, gain):
    inner = grad * gain
    first = jnp.mean(inner, axis=-1, keepdims=True)
    second = jnp.mean(inner * scaled, axis=-1, keepdims=True)
    return inverse * (inner - first - scaled * second)


class Spread:
    def __init__(self, at, full, send, recv):
        self.at, self.full, self.send, self.recv = at, full, send, recv
        self.rows = full.shape[0] // 4
        self.step = self.rows // CHUNKS

    def block(self, k, i):
        return self.full.at[pl.ds(k * self.rows + i * self.step, self.step)]

    def side(self, i):
        return remote(self.block(0, i), self.block(1, i), self.send.at[0, i], self.recv.at[0, i], self.at["core"])

    def far(self, i):
        return remote(self.block(0, i), self.block(2, i), self.send.at[1, i], self.recv.at[1, i], self.at["near"])

    def onward(self, i):
        return remote(self.block(2, i), self.block(3, i), self.send.at[2, i], self.recv.at[2, i], self.at["core"])

    def post(self, i):
        self.far(i).start()
        self.side(i).start()

    def forward(self, i):
        self.far(i).wait_recv()
        self.onward(i).start()

    def finish(self):
        for i in range(CHUNKS):
            self.side(i).wait()
            self.far(i).wait_send()
            self.onward(i).wait()


class Gathered:
    def __init__(self, at, part, side, far, mix, send, recv):
        self.at, self.part, self.side, self.far, self.mix = at, part, side, far, mix
        self.send, self.recv = send, recv
        self.rows = part.shape[0] // 4
        self.step = self.rows // CHUNKS

    def away(self, i):
        src = self.part.at[pl.ds(3 * self.rows + i * self.step, self.step)]
        dst = self.side.at[pl.ds(self.rows + i * self.step, self.step)]
        return remote(src, dst, self.send.at[0, i], self.recv.at[0, i], self.at["core"])

    def home(self, i):
        src = self.part.at[pl.ds(self.rows + i * self.step, self.step)]
        dst = self.side.at[pl.ds(i * self.step, self.step)]
        return remote(src, dst, self.send.at[1, i], self.recv.at[1, i], self.at["core"])

    def over(self, i):
        here = pl.ds(i * self.step, self.step)
        return remote(self.mix.at[here], self.far.at[here], self.send.at[2, i], self.recv.at[2, i], self.at["near"])

    def begin(self):
        for i in range(CHUNKS):
            self.away(i).start()
        for i in range(CHUNKS):
            self.home(i).start()
        for i in range(CHUNKS):
            self.away(i).wait_recv()
            here = pl.ds(i * self.step, self.step)
            ours = self.part[pl.ds(2 * self.rows + i * self.step, self.step)].astype(F32)
            theirs = self.side[pl.ds(self.rows + i * self.step, self.step)].astype(F32)
            self.mix[here] = (ours + theirs).astype(BF16)
            self.over(i).start()

    def take(self, i):
        self.home(i).wait_recv()
        self.over(i).wait_recv()
        here = pl.ds(i * self.step, self.step)
        return self.part[here].astype(F32) + self.side[here].astype(F32) + self.far[here].astype(F32)

    def finish(self):
        for i in range(CHUNKS):
            self.away(i).wait_send()
            self.home(i).wait_send()
            self.over(i).wait_send()


def sems(*shape):
    return [pltpu.SemaphoreType.DMA(shape), pltpu.SemaphoreType.DMA(shape)]


def comm_params(number, mib=56):
    return pltpu.CompilerParams(collective_id=number, has_side_effects=True, vmem_limit_bytes=mib << 20)


VMEM_SPEC = pl.BlockSpec(memory_space=pltpu.VMEM)
ANY_SPEC = pl.BlockSpec(memory_space=pl.ANY)


def enter_kernel(tokens, w, gain, shift, full, tok, role, ts, tr, gs, gr, ws, wr, bs, br, local):
    at = places()
    moved = at["moved"]
    still = jnp.logical_not(moved)
    rows = tokens.shape[0]
    step = rows // CHUNKS
    peers = (at["left"], at["up"], at["both"])
    size = w.shape[1] // 4
    piece = pl.ds(pl.multiple_of(at["line"] * size, size), size)
    greet((at["core"], at["near"]), (at["cross"],) + peers, moved)

    def token(i):
        here = pl.ds(i * step, step)
        return remote(tokens.at[here], tok.at[here], ts.at[i], tr.at[i], at["cross"])

    def cross(j):
        return remote(w.at[j, piece], role.at[j, piece], ws.at[j], wr.at[j], at["cross"])

    def share(j, k):
        return remote(role.at[j, piece], role.at[j, piece], bs.at[j, k], br.at[j, k], peers[k])

    def own(j):
        return pltpu.make_async_copy(w.at[j], role.at[j], local.at[j])

    @pl.when(moved)
    def _():
        for i in range(CHUNKS):
            token(i).start()

    @pl.when(still)
    def _():
        tok[...] = tokens[...]
        for j in range(3):
            own(j).start()

    spread = Spread(at, full, gs, gr)
    for i in range(CHUNKS):
        here = slice(i * step, (i + 1) * step)

        @pl.when(moved)
        def _():
            token(i).wait_recv()

        unit, _ = unit_rows(tok[here].astype(F32))
        full[here] = (unit * gain[...] + shift[...]).astype(BF16)
        spread.post(i)

    @pl.when(moved)
    def _():
        for j in range(3):
            cross(j).start()

    for i in range(CHUNKS):
        spread.forward(i)

    @pl.when(moved)
    def _():
        for j in range(3):
            cross(j).wait_recv()
            for k in range(3):
                share(j, k).start()
        for i in range(CHUNKS):
            token(i).wait_send()
        for j in range(3):
            cross(j).wait_send()
            for k in range(3):
                share(j, k).wait()

    @pl.when(still)
    def _():
        for j in range(3):
            own(j).wait()

    spread.finish()


def enter(tokens, w3, gain, shift):
    rows, width = tokens.shape
    return pl.pallas_call(
        enter_kernel,
        in_specs=[VMEM_SPEC, ANY_SPEC, VMEM_SPEC, VMEM_SPEC],
        out_specs=[VMEM_SPEC, VMEM_SPEC, ANY_SPEC],
        out_shape=[
            jax.ShapeDtypeStruct((4 * rows, width), BF16),
            jax.ShapeDtypeStruct((rows, width), BF16),
            jax.ShapeDtypeStruct(w3.shape, BF16),
        ],
        scratch_shapes=sems(CHUNKS) + sems(3, CHUNKS) + sems(3) + sems(3, 3) + [pltpu.SemaphoreType.DMA((3,))],
        compiler_params=comm_params(1, 24),
        name="enter",
    )(tokens, w3, gain, shift)


def middle_kernel(part, tok, bias, gain, shift, full, mid, side, far, mix, rs, rr, gs, gr):
    at = places()
    greet((at["core"], at["near"]))
    step = tok.shape[0] // CHUNKS
    total = Gathered(at, part, side, far, mix, rs, rr)
    spread = Spread(at, full, gs, gr)
    total.begin()
    for i in range(CHUNKS):
        here = slice(i * step, (i + 1) * step)
        value = tok[here].astype(F32) + (total.take(i) + bias[...])
        mid[here] = value
        unit, _ = unit_rows(value)
        full[here] = (unit * gain[...] + shift[...]).astype(BF16)
        spread.post(i)
    for i in range(CHUNKS):
        spread.forward(i)
    total.finish()
    spread.finish()


def middle_rows(part, tok, bias, gain, shift):
    rows, width = tok.shape
    return pl.pallas_call(
        middle_kernel,
        in_specs=[VMEM_SPEC] * 5,
        out_specs=[VMEM_SPEC] * 2,
        out_shape=[jax.ShapeDtypeStruct((4 * rows, width), BF16), jax.ShapeDtypeStruct((rows, width), F32)],
        scratch_shapes=[VM((2 * rows, width), BF16), VM((rows, width), BF16), VM((rows, width), BF16)]
        + sems(3, CHUNKS) + sems(3, CHUNKS),
        compiler_params=comm_params(2, 40),
        name="middle_rows",
    )(part, tok, bias, gain, shift)


def turn_kernel(part, cot, mid, gain, full, grad, side, far, mix, rs, rr, gs, gr):
    at = places()
    greet((at["core"], at["near"]))
    step = cot.shape[0] // CHUNKS
    total = Gathered(at, part, side, far, mix, rs, rr)
    spread = Spread(at, full, gs, gr)
    total.begin()
    for i in range(CHUNKS):
        here = slice(i * step, (i + 1) * step)
        unit, inverse = unit_rows(mid[here])
        value = cot[here].astype(F32) + unit_back(total.take(i), unit, inverse, gain[...])
        grad[here] = value
        full[here] = value.astype(BF16)
        spread.post(i)
    for i in range(CHUNKS):
        spread.forward(i)
    total.finish()
    spread.finish()


def turn_rows(part, cot, mid, gain):
    rows, width = cot.shape
    return pl.pallas_call(
        turn_kernel,
        in_specs=[VMEM_SPEC] * 4,
        out_specs=[VMEM_SPEC] * 2,
        out_shape=[jax.ShapeDtypeStruct((4 * rows, width), BF16), jax.ShapeDtypeStruct((rows, width), F32)],
        scratch_shapes=[VM((2 * rows, width), BF16), VM((rows, width), BF16), VM((rows, width), BF16)]
        + sems(3, CHUNKS) + sems(3, CHUNKS),
        compiler_params=comm_params(3, 40),
        name="turn_rows",
    )(part, cot, mid, gain)


def leave_kernel(part, tok, grad, gain, out, side, far, mix, done, rs, rr, os, orr):
    at = places()
    moved = at["moved"]
    greet((at["core"], at["near"]), (at["cross"],), moved)
    step = tok.shape[0] // CHUNKS
    total = Gathered(at, part, side, far, mix, rs, rr)

    def back(i):
        here = pl.ds(i * step, step)
        return remote(done.at[here], out.at[here], os.at[i], orr.at[i], at["cross"])

    total.begin()
    for i in range(CHUNKS):
        here = slice(i * step, (i + 1) * step)
        unit, inverse = unit_rows(tok[here].astype(F32))
        value = (grad[here] + unit_back(total.take(i), unit, inverse, gain[...])).astype(BF16)

        @pl.when(moved)
        def _():
            done[here] = value
            back(i).start()

        @pl.when(jnp.logical_not(moved))
        def _():
            out[here] = value

    total.finish()

    @pl.when(moved)
    def _():
        for i in range(CHUNKS):
            back(i).wait()


def leave(part, tok, grad, gain):
    rows, width = tok.shape
    return pl.pallas_call(
        leave_kernel,
        in_specs=[VMEM_SPEC] * 4,
        out_specs=VMEM_SPEC,
        out_shape=jax.ShapeDtypeStruct((rows, width), BF16),
        scratch_shapes=[
            VM((2 * rows, width), BF16), VM((rows, width), BF16), VM((rows, width), BF16), VM((rows, width), BF16)
        ] + sems(3, CHUNKS) + sems(CHUNKS),
        compiler_params=comm_params(4, 40),
        name="leave",
    )(part, tok, grad, gain)


def routes(nd, nt):
    def lin(d, t):
        return d * nt + t

    every = [(d, t) for d in range(nd) for t in range(nt)]
    moved = [(d, t) for d, t in every if (d & 1) != (t >> 1)]
    both = [(lin(d, t), lin(d ^ 1, t ^ 2)) for d, t in moved]
    return dict(
        swap=both + [(lin(d, t), lin(d, t)) for d, t in every if (d & 1) == (t >> 1)],
        cross=both,
        core=[(lin(d, t), lin(d ^ 1, t)) for d, t in every],
        near=[(lin(d, t), lin(d, t ^ 1)) for d, t in every],
        left=[(lin(d, t), lin(d ^ 2, t)) for d, t in moved],
        up=[(lin(d, t), lin(d ^ 4, t)) for d, t in moved],
    )


def pick(table, e):
    return lax.dynamic_index_in_dim(table, e, 0, keepdims=False)


def norm_rows(values):
    centre = values - jnp.mean(values, axis=-1, keepdims=True)
    inverse = lax.rsqrt(jnp.mean(centre * centre, axis=-1, keepdims=True) + EPS)
    return centre * inverse, inverse


def norm_back(grad_rows, scaled, inverse, gain_row):
    inner = grad_rows * gain_row
    first = jnp.mean(inner, axis=-1, keepdims=True)
    second = jnp.mean(inner * scaled, axis=-1, keepdims=True)
    return inverse * (inner - first - scaled * second)


def body(
    tokens, cotangent, norm_gains, norm_shifts, query_key_value_weight, b_qv, output_weight,
    output_bias_vector, up_weight, b_up, down_weight, down_bias_vector, adapter_query_key_value_input,
    qkv_out, adapter_output_input, adapter_output_output, adapter_up_input, up_out, down_in,
    adapter_down_output, offsets, adapter_ids,
):
    nd, nt = lax.axis_size("dp"), lax.axis_size("tensor")
    route = routes(nd, nt)
    d, t = lax.axis_index("dp"), lax.axis_index("tensor")
    c, p = d % 2, (d // 2) % 4
    moved = c != t // 2
    me = 2 * c + t % 2
    rows, width = tokens.shape
    length = rows * nt
    local = output_weight.shape[0]
    local_heads = local // HEAD_DIM
    hidden_width = up_weight.shape[1]
    rank = adapter_up_input.shape[1]
    tables = adapter_up_input.shape[0]

    def go(x, name):
        return lax.ppermute(x, AXES, route[name])

    ids = adapter_ids[0]
    w3 = jnp.transpose(query_key_value_weight, (1, 0, 2))
    b3 = jnp.transpose(qkv_out, (0, 2, 1, 3))
    small = jnp.concatenate(
        [
            jnp.transpose(pick(b3, ids[0]), (1, 0, 2)).reshape(rank, 3 * local),
            pick(adapter_output_input, ids[1]),
            pick(up_out, ids[2]),
            pick(down_in, ids[3]),
        ],
        1,
    )
    small = go(small, "swap")
    biases = go(jnp.concatenate([b_qv.reshape(1, 2 * local), b_up.reshape(1, hidden_width)], 1), "swap")
    numbers = go(jnp.concatenate([offsets, adapter_ids], 1), "swap")
    cuts = [3 * local, 4 * local, 4 * local + hidden_width]
    bq, ao, bu, ad = jnp.split(small, cuts, 1)
    bias_q, bias_v, bias_up = jnp.split(biases, [local, 2 * local], 1)
    own_ids = numbers[0, 2:6]
    aq = pick(adapter_query_key_value_input, own_ids[0])
    bo = pick(adapter_output_output, own_ids[1])
    au = pick(adapter_up_input, own_ids[2])
    bd = pick(adapter_down_output, own_ids[3])

    def bring(weight, axis):
        size = weight.shape[axis] // 4
        r0 = go(lax.dynamic_slice_in_dim(weight, p * size, size, axis), "cross")
        r1 = go(r0, "left")
        r2 = go(r0, "up")
        r3 = go(r1, "up")
        parts = [r0, r1, r2, r3]
        whole = []
        for j in range(4):
            part = parts[j]
            for q in range(1, 4):
                part = jnp.where(p == q, parts[j ^ q], part)
            whole.append(part)
        return jnp.where(moved, jnp.concatenate(whole, axis), weight)

    gain = [norm_gains[i : i + 1] for i in range(2)]
    shift = [norm_shifts[i : i + 1] for i in range(2)]
    x, tok, wqkv = enter(tokens, w3, gain[0], shift[0])
    output_weight, up_weight, down_weight, cotangent, _ = lax.optimization_barrier(
        (output_weight, up_weight, down_weight, cotangent, x)
    )
    cot_own = go(cotangent, "swap")
    wo = bring(output_weight, 0)
    wu = bring(up_weight, 1)
    wd = bring(down_weight, 0)

    def gather(own):
        far = go(own, "near")
        side = go(own, "core")
        last = go(far, "core")
        return own, side, far, last

    def scatter(home, away):
        far = (away[:rows].astype(F32) + go(away[rows:], "core").astype(F32)).astype(BF16)
        far = go(far, "near")
        side = go(home[rows:], "core")
        return home[:rows].astype(F32) + side.astype(F32) + far.astype(F32)

    def wide(a):
        return jnp.pad(a, ((0, PAD - rank), (0, 0)))

    ints = jnp.concatenate([jnp.reshape(me, (1,)).astype(jnp.int32), numbers[0, 0:2]])
    head_ids = (me * local_heads + jnp.arange(local_heads, dtype=jnp.int32)).astype(F32)
    slopes = jnp.exp2(-8.0 * (head_ids + 1.0) / HEADS)
    bq, ao, bu, ad, aq, bo, au, bd = [wide(a) for a in (bq, ao, bu, ad, aq, bo, au, bd)]

    qkv_bias = jnp.concatenate([bias_q, jnp.zeros_like(bias_q), bias_v], 1)
    proj, rank_qkv = fwd_qkv(x, wqkv, aq, bq, qkv_bias)
    ctx, lse = attend(ints, slopes, proj, rows)
    part, rank_out = fwd_o(ctx, wo, ao, bo, rows)
    nm, middle = middle_rows(part, tok, output_bias_vector.reshape(1, width), gain[1], shift[1])
    n0, n1, n2, n3 = [nm[i * rows : (i + 1) * rows] for i in range(4)]
    c0, c1, c2, c3 = gather(cot_own)
    tile = hidden_width // 4
    p0, q0, tuo0, tdi0, tui0, tdo0 = mlp(n0, n1, c0, c1, wu, wd, au, bu, ad, bd, bias_up, tile)
    p1, q1, tuo1, tdi1, tui1, tdo1 = mlp(n2, n3, c2, c3, wu, wd, au, bu, ad, bd, bias_up, tile)
    t_up_out, t_down_in, t_up_in, t_down_out = tuo0 + tuo1, tdi0 + tdi1, tui0 + tui1, tdo0 + tdo1
    gm, grad_middle = turn_rows(jnp.concatenate([q0, q1], 0), cot_own, middle, gain[1])
    result = (middle + (scatter(p0, p1) + down_bias_vector)).astype(BF16)
    grad_ctx, t_out_out, t_out_in = bwd_o(gm, wo, bo, ao, rank_out, ctx, rows)
    grad_proj = attend_back(ints, slopes, proj, grad_ctx, lse, rows)
    gx, t_qkv_out, t_qkv_in = bwd_qkv(grad_proj, wqkv, bq, aq, rank_qkv, x, rows)
    in_grad = leave(gx, tok, grad_middle, gain[0])

    result = go(result, "swap")

    def owned(pieces):
        return lax.all_gather(go(jnp.concatenate(pieces, 1).astype(BF16), "swap"), "dp", axis=0)

    everyone = lax.all_gather(adapter_ids, "dp", axis=0, tiled=True)
    hot = (everyone[:, :, None] == jnp.arange(tables, dtype=jnp.int32)).astype(BF16)

    def combine(per, which):
        return jnp.einsum("se,srm->erm", hot[:, which], per, preferred_element_type=F32)

    own = owned([t[:rank] for t in (t_qkv_out, t_out_in, t_up_out, t_down_in)])
    g_qkv_out = jnp.einsum(
        "se,srkm->erkm", hot[:, 0], own[:, :, : cuts[0]].reshape(nd, rank, 3, local), preferred_element_type=F32
    )
    g_out_in = combine(own[:, :, cuts[0] : cuts[1]], 1)
    g_up_out = combine(own[:, :, cuts[1] : cuts[2]], 2)
    g_down_in = combine(own[:, :, cuts[2] :], 3)

    shared = jnp.stack([t[:rank] for t in (t_qkv_in, t_out_out, t_up_in, t_down_out)]).astype(BF16)
    shared = shared.astype(F32) + go(shared, "core").astype(F32)
    shared = (shared + go(shared.astype(BF16), "near").astype(F32)).astype(BF16)
    quarter = width // 4
    mine = lax.dynamic_slice_in_dim(shared, me * quarter, quarter, 2)
    mine = go(mine, "swap")
    mine = lax.all_gather(mine, "dp", axis=0)
    sums = jnp.einsum("ske,skrm->kerm", hot.transpose(0, 1, 2), mine, preferred_element_type=F32)
    whole = lax.all_gather(sums.astype(BF16), "tensor", axis=3, tiled=True).astype(F32)
    return (
        result, in_grad, whole[0], g_qkv_out, g_out_in, whole[1], whole[2], g_up_out, g_down_in, whole[3],
    )


def solution(mesh):
    placed = (
        P(("dp", "tensor"), None), P(("dp", "tensor"), None), P(), P(), P(None, None, "tensor"), P(None, "tensor"),
        P("tensor", None), P(), P(None, "tensor"), P("tensor"), P("tensor", None), P(), P(),
        P(None, None, None, "tensor"), P(None, None, "tensor"), P(), P(), P(None, None, "tensor"),
        P(None, None, "tensor"), P(), P("dp", None), P("dp", None),
    )
    return jax.shard_map(
        body, mesh=mesh, in_specs=placed,
        out_specs=(
            P(("dp", "tensor"), None), P(("dp", "tensor"), None), P(), P(None, None, None, "tensor"),
            P(None, None, "tensor"), P(), P(), P(None, None, "tensor"), P(None, None, "tensor"), P(),
        ),
        check_vma=False,
    )
```

```python
import functools
import math

import jax
import jax.numpy as jnp
from jax import lax
from jax.experimental import pallas as pl
from jax.experimental.pallas import tpu as pltpu
from jax.sharding import PartitionSpec as P

HEADS = 16
HEAD_DIM = 128
PIECE = 256
ITEM = 128
AHEAD = 3
EPS = 1e-05
GELU_C = 0.7978845608028654
GELU_K = 0.044715
LOG2E = 1.4426950408889634
FAR = 1e32
F32 = jnp.float32
BF16 = jnp.bfloat16
AXES = ("dp", "tensor")
VM = pltpu.VMEM
HERE = pl.BlockSpec(memory_space=pl.ANY)


def dot(a, b):
    return lax.dot_general(a, b, (((1,), (0,)), ((), ())), preferred_element_type=F32)


def dot_t(a, b):
    return lax.dot_general(a, b, (((1,), (1,)), ((), ())), preferred_element_type=F32)


def t_dot(a, b):
    return lax.dot_general(a, b, (((0,), (0,)), ((), ())), preferred_element_type=F32)


def whole(shape):
    zeros = (0,) * len(shape)
    return pl.BlockSpec(shape, lambda *_: zeros)


def params(mib=56):
    return pltpu.CompilerParams(vmem_limit_bytes=mib << 20)


def cost(flops, read):
    return pl.CostEstimate(flops=int(flops), bytes_accessed=int(read), transcendentals=0)


def displaced():
    return (lax.axis_index("dp") % 2 + lax.axis_index("tensor") // 2) % 2 == 1


def fetch(native, brought, into, sem):
    moved = displaced()

    @pl.when(moved)
    def _():
        pltpu.make_async_copy(brought, into, sem).start()

    @pl.when(jnp.logical_not(moved))
    def _():
        pltpu.make_async_copy(native, into, sem).start()

    return pltpu.make_async_copy(native, into, sem)


def bwd_o_kernel(g, native, brought, b, a, rank, x, out, tb, ta, w, sem):
    first = pl.program_id(0) == 0

    @pl.when(first)
    def _():
        fetch(native, brought, w, sem).wait()

    r = dot_t(g[...], b[...]).astype(BF16)
    out[...] = (dot_t(g[...], w[...]) + dot(r, a[...])).astype(BF16)
    one = t_dot(rank[...], g[...])
    two = t_dot(r, x[...])

    @pl.when(first)
    def _():
        tb[...] = one
        ta[...] = two

    @pl.when(jnp.logical_not(first))
    def _():
        tb[...] += one
        ta[...] += two


def bwd_o(g, w, brought, chosen, small, rank, x, tile):
    n, k = g.shape
    cols = w.shape[0]
    low = rank.shape[1]
    row = lambda c: pl.BlockSpec((tile, c), lambda i: (i, 0))
    return pl.pallas_call(
        bwd_o_kernel,
        grid=(n // tile,),
        in_specs=[row(k), HERE, HERE, pl.BlockSpec((low, k), lambda i: (1, 0)), pl.BlockSpec((low, cols), lambda i: (0, 3)), row(low), row(cols)],
        out_specs=[row(cols), whole((low, k)), whole((low, cols))],
        out_shape=[
            jax.ShapeDtypeStruct((n, cols), BF16),
            jax.ShapeDtypeStruct((low, k), F32),
            jax.ShapeDtypeStruct((low, cols), F32),
        ],
        scratch_shapes=[VM(w.shape, BF16), pltpu.SemaphoreType.DMA],
        compiler_params=params(),
        cost_estimate=cost(2 * n * k * cols, 2 * (n * k + k * cols + n * cols)),
        name="bwd_o",
    )(g, w, brought, chosen, small, rank, x)


def bwd_qkv_kernel(g, native, brought, b, a, rank, x, out, tb, ta, w, sem):
    first = pl.program_id(0) == 0

    @pl.when(first)
    def _():
        fetch(native, brought, w, sem).wait()

    cols = w.shape[2]
    r = dot_t(g[...], b[...]).astype(BF16)
    acc = dot(r, a[...])
    for j in range(3):
        acc = acc + dot_t(g[:, j * cols : (j + 1) * cols], w[j])
    out[...] = acc.astype(BF16)
    one = t_dot(rank[...], g[...])
    two = t_dot(r, x[...])

    @pl.when(first)
    def _():
        tb[...] = one
        ta[...] = two

    @pl.when(jnp.logical_not(first))
    def _():
        tb[...] += one
        ta[...] += two


def bwd_qkv(g, w3, brought, small, chosen, rank, x, tile):
    n, k = g.shape
    cols = w3.shape[1]
    low = rank.shape[1]
    row = lambda c: pl.BlockSpec((tile, c), lambda i: (i, 0))
    return pl.pallas_call(
        bwd_qkv_kernel,
        grid=(n // tile,),
        in_specs=[row(k), HERE, HERE, pl.BlockSpec((low, k), lambda i: (0, 0)), pl.BlockSpec((low, cols), lambda i: (0, 0)), row(low), row(cols)],
        out_specs=[row(cols), whole((low, k)), whole((low, cols))],
        out_shape=[
            jax.ShapeDtypeStruct((n, cols), BF16),
            jax.ShapeDtypeStruct((low, k), F32),
            jax.ShapeDtypeStruct((low, cols), F32),
        ],
        scratch_shapes=[VM(w3.shape, BF16), pltpu.SemaphoreType.DMA],
        compiler_params=params(),
        cost_estimate=cost(2 * n * k * cols, 2 * (n * k + k * cols + n * cols)),
        name="bwd_qkv",
    )(g, w3, brought, small, chosen, rank, x)


def distances(me, s0, s1, rows, step, dist):
    length = dist.shape[0]

    def piece(pos, none):
        one = jnp.where((pos >= s0) & (pos < s0 + PIECE), 1.0, none)
        return jnp.where((pos >= s1) & (pos < s1 + PIECE), 2.0, one)

    def rel(j):
        return ((j & 1) << 1) | (j >> 1)

    i = lax.broadcasted_iota(jnp.int32, (length, 128), 0)
    kpos = ((me ^ rel(i // rows)) * rows + i % rows).astype(F32)[:, :1]
    qpos = ((me ^ rel(step)) * rows + lax.broadcasted_iota(jnp.int32, (1, rows), 1)).astype(F32)
    seen = (kpos <= qpos) | (piece(kpos, -1.0) == piece(qpos, -2.0))
    dist[...] = jnp.where(seen, jnp.abs(kpos - qpos), FAR)


def head_slopes(me, heads):
    first = jnp.full((1, 1), me * heads, jnp.int32).astype(F32)
    return [jnp.exp2((first + float(h + 1)) * (-8.0 / HEADS)) * LOG2E for h in range(heads)]


def attend_back_kernel(nums, q, k, v, g, lse, out, dist, kt, gk, gv):
    step = pl.program_id(0)
    rows = q.shape[0]
    local = q.shape[1]
    heads = local // HEAD_DIM
    scale = 1.0 / math.sqrt(HEAD_DIM)
    me = 2 * (lax.axis_index("dp") % 2) + lax.axis_index("tensor") % 2
    base = nums.shape[1] - 128
    distances(me, nums[0:1, base : base + 1], nums[0:1, base + 1 : base + 2], rows, step, dist)
    slopes = head_slopes(me, heads)

    @pl.when(step == 0)
    def _():
        kt[...] = k[...].T
        gk[...] = jnp.zeros_like(gk)
        gv[...] = jnp.zeros_like(gv)

    at = pl.ds(pl.multiple_of(step * rows, rows), rows)
    for h in range(heads):
        span = slice(h * HEAD_DIM, (h + 1) * HEAD_DIM)
        s = dot_t(k[:, span], q[:, span]) * (scale * LOG2E) - dist[...] * slopes[h]
        p = jnp.exp2(s - lse[h : h + 1, :])
        gv[:, span] += dot(p.astype(BF16), g[:, span])
        gp = dot_t(v[:, span], g[:, span])
        inner = jnp.sum(p * gp, axis=0, keepdims=True)
        gs = (p * (gp - inner)).astype(BF16)
        gk[:, span] += dot(gs, q[:, span])
        out[at, span] = (dot(kt[span, :], gs).T * scale).astype(BF16)

    @pl.when(step == pl.num_programs(0) - 1)
    def _():
        out[:, local : 2 * local] = (gk[...] * scale).astype(BF16)
        out[:, 2 * local :] = gv[...].astype(BF16)


def attend_back(nums, proj, g, lse, rows):
    length, three = proj.shape
    local = three // 3
    heads = local // HEAD_DIM
    return pl.pallas_call(
        attend_back_kernel,
        grid=(length // rows,),
        in_specs=[
            whole(nums.shape),
            pl.BlockSpec((rows, local), lambda i: (i, 0)),
            pl.BlockSpec((length, local), lambda i: (0, 1)),
            pl.BlockSpec((length, local), lambda i: (0, 2)),
            pl.BlockSpec((rows, local), lambda i: (i, 0)),
            pl.BlockSpec((heads, rows), lambda i: (0, i)),
        ],
        out_specs=pl.BlockSpec((length, three), lambda i: (0, 0)),
        scratch_shapes=[
            VM((length, rows), F32), VM((local, length), BF16), VM((length, local), F32), VM((length, local), F32),
        ],
        out_shape=jax.ShapeDtypeStruct((length, three), BF16),
        compiler_params=params(),
        cost_estimate=cost(10 * length * length * local, 16 * length * local),
        name="attend_back",
    )(nums, proj, proj, proj, g, lse)


def gelu_parts(values):
    square = values * values
    tangent = jnp.tanh(GELU_C * (values + GELU_K * square * values))
    half = 0.5 * (1.0 + tangent)
    slope = half + (0.5 * GELU_C) * values * (1.0 - tangent * tangent) * (1.0 + 3.0 * GELU_K * square)
    return values * half, slope


def mlp_kernel(
    nm, cot, wu_native, wu_brought, wd_native, wd_brought, au, bu, ad, bd, bias, part, back, tuo, tdi, tui, tdo,
    up_rank, down_rank, g_up, g_down, acc, gacc, wu_slots, wd_slots, sem,
):
    step, half = pl.program_id(0), pl.program_id(1)
    last = pl.num_programs(0) - 1
    rows = nm.shape[0]
    tile = bu.shape[1]

    def load(j):
        slot = j % 2
        cut = pl.ds(pl.multiple_of(j * tile, tile), tile)
        return (
            fetch(wu_native.at[:, cut], wu_brought.at[:, cut], wu_slots.at[slot], sem.at[0, slot]),
            fetch(wd_native.at[cut], wd_brought.at[cut], wd_slots.at[slot], sem.at[1, slot]),
        )

    def await_slot(slot):
        pltpu.make_async_copy(wu_native.at[:, pl.ds(0, tile)], wu_slots.at[slot], sem.at[0, slot]).wait()
        pltpu.make_async_copy(wd_native.at[pl.ds(0, tile)], wd_slots.at[slot], sem.at[1, slot]).wait()

    @pl.when((step == 0) & (half == 0))
    def _():
        load(step)

    @pl.when(half == 0)
    def _():
        await_slot(step % 2)

        @pl.when(step < last)
        def _():
            load(step + 1)

    wu = wu_slots.at[step % 2]
    wd = wd_slots.at[step % 2]
    here = pl.ds(pl.multiple_of(half * rows, rows), rows)

    @pl.when(step == 0)
    def _():
        up_rank[here] = dot_t(nm[...], au[...]).astype(BF16)
        g_down[here] = dot_t(cot[...], bd[...]).astype(BF16)
        down_rank[here] = jnp.zeros((rows, au.shape[0]), F32)
        g_up[here] = jnp.zeros((rows, au.shape[0]), F32)
        acc[here] = jnp.zeros((rows, nm.shape[1]), F32)
        gacc[here] = jnp.zeros((rows, nm.shape[1]), F32)

    gate = dot(nm[...], wu[...]) + dot(up_rank[here], bu[...]) + bias[...]
    value, slope = gelu_parts(gate)
    hidden = value.astype(BF16)
    grad = dot_t(cot[...], wd[...]) + dot(g_down[here], ad[...])
    grad_gate = (grad * slope).astype(BF16)
    down_rank[here] += dot_t(hidden, ad[...])
    g_up[here] += dot_t(grad_gate, bu[...])
    acc[here] += dot(hidden, wd[...])
    gacc[here] += dot_t(grad_gate, wu[...])
    one = t_dot(up_rank[here], grad_gate)
    two = t_dot(g_down[here], hidden)

    @pl.when(half == 0)
    def _():
        tuo[...] = one
        tdi[...] = two

    @pl.when(half > 0)
    def _():
        tuo[...] += one
        tdi[...] += two

    @pl.when(step == last)
    def _():
        dr = down_rank[here].astype(BF16)
        gu = g_up[here].astype(BF16)
        part[...] = (acc[here] + dot(dr, bd[...])).astype(BF16)
        back[...] = (gacc[here] + dot(gu, au[...])).astype(BF16)
        three = t_dot(gu, nm[...])
        four = t_dot(dr, cot[...])

        @pl.when(half == 0)
        def _():
            tui[...] = three
            tdo[...] = four

        @pl.when(half > 0)
        def _():
            tui[...] += three
            tdo[...] += four


def mlp(nm, cot, wu, wu_brought, wd, wd_brought, chosen, small, nums, tile):
    n, width = nm.shape
    rows = n // 2
    hidden = wu.shape[1]
    last = hidden // tile - 1
    low = small.shape[0]
    first = (small.shape[1] - 2 * hidden) // tile
    bias_first = (nums.shape[1] - 128 - hidden) // tile
    cut = lambda r: pl.BlockSpec((r, tile), lambda j, i: (0, j))
    row = pl.BlockSpec((rows, width), lambda j, i: (i, 0))
    result = pl.BlockSpec((rows, width), lambda j, i: (jnp.where(j == last, i, 0), 0))
    return pl.pallas_call(
        mlp_kernel,
        grid=(hidden // tile, 2),
        in_specs=[
            row, row, HERE, HERE, HERE, HERE,
            pl.BlockSpec((low, width), lambda j, i: (2, 0)),
            pl.BlockSpec((low, tile), lambda j, i: (0, first + j)),
            pl.BlockSpec((low, tile), lambda j, i: (0, first + hidden // tile + j)),
            pl.BlockSpec((low, width), lambda j, i: (3, 0)),
            pl.BlockSpec((1, tile), lambda j, i: (0, bias_first + j)),
        ],
        out_specs=[result, result, cut(low), cut(low), whole((low, width)), whole((low, width))],
        out_shape=[
            jax.ShapeDtypeStruct((n, width), BF16),
            jax.ShapeDtypeStruct((n, width), BF16),
            jax.ShapeDtypeStruct((low, hidden), F32),
            jax.ShapeDtypeStruct((low, hidden), F32),
            jax.ShapeDtypeStruct((low, width), F32),
            jax.ShapeDtypeStruct((low, width), F32),
        ],
        scratch_shapes=[
            VM((n, low), BF16), VM((n, low), F32), VM((n, low), F32), VM((n, low), BF16),
            VM((n, width), F32), VM((n, width), F32),
            VM((2, width, tile), BF16), VM((2, tile, width), BF16), pltpu.SemaphoreType.DMA((2, 2)),
        ],
        compiler_params=params(60),
        cost_estimate=cost(8 * n * width * hidden, 4 * width * hidden + 12 * n * width),
        name="mlp",
    )(nm, cot, wu, wu_brought, wd, wd_brought, chosen, small, small, chosen, nums)


MESH = pl.DeviceIdType.MESH
CHUNKS = 4


def places():
    d, t = lax.axis_index("dp"), lax.axis_index("tensor")
    core, zh = d % 2, t // 2
    core_d = d + 1 - 2 * core
    near_t = t + 1 - 2 * (t % 2)
    left = d + 2 - 4 * ((d // 2) % 2)
    up = 4 - 8 * ((d // 4) % 2)
    return dict(
        moved=(core + zh) % 2 == 1,
        line=(d // 2) % 4,
        core=(core_d, t),
        near=(d, near_t),
        cross=(core_d, t + 2 - 4 * zh),
        left=(left, t),
        up=(d + up, t),
        both=(left + up, t),
    )


def greet(always, sometimes=(), when=None):
    barrier = pltpu.get_barrier_semaphore()
    for peer in always:
        pl.semaphore_signal(barrier, inc=1, device_id=peer, device_id_type=MESH)
    count = len(always)
    if sometimes:

        @pl.when(when)
        def _():
            for peer in sometimes:
                pl.semaphore_signal(barrier, inc=1, device_id=peer, device_id_type=MESH)

        count = count + len(sometimes) * when.astype(jnp.int32)
    pl.semaphore_wait(barrier, count)


def remote(src, dst, send, recv, peer):
    return pltpu.make_async_remote_copy(
        src_ref=src, dst_ref=dst, send_sem=send, recv_sem=recv, device_id=peer, device_id_type=MESH
    )


def unit_rows(v):
    centre = v - jnp.mean(v, axis=-1, keepdims=True)
    inverse = lax.rsqrt(jnp.mean(centre * centre, axis=-1, keepdims=True) + EPS)
    return centre * inverse, inverse


def unit_back(grad, scaled, inverse, gain):
    inner = grad * gain
    first = jnp.mean(inner, axis=-1, keepdims=True)
    second = jnp.mean(inner * scaled, axis=-1, keepdims=True)
    return inverse * (inner - first - scaled * second)


class Spread:
    def __init__(self, at, full, send, recv):
        self.at, self.full, self.send, self.recv = at, full, send, recv
        self.rows = full.shape[0] // 4
        self.step = self.rows // CHUNKS

    def block(self, k, i):
        return self.full.at[pl.ds(k * self.rows + i * self.step, self.step)]

    def side(self, i):
        return remote(self.block(0, i), self.block(1, i), self.send.at[0, i], self.recv.at[0, i], self.at["core"])

    def far(self, i):
        return remote(self.block(0, i), self.block(2, i), self.send.at[1, i], self.recv.at[1, i], self.at["near"])

    def onward(self, i):
        return remote(self.block(2, i), self.block(3, i), self.send.at[2, i], self.recv.at[2, i], self.at["core"])

    def post(self, i):
        self.far(i).start()
        self.side(i).start()

    def forward(self, i):
        self.far(i).wait_recv()
        self.onward(i).start()

    def finish(self):
        for i in range(CHUNKS):
            self.side(i).wait()
            self.far(i).wait_send()
            self.onward(i).wait()


class Gathered:
    def __init__(self, at, part, side, far, mix, send, recv):
        self.at, self.part, self.side, self.far, self.mix = at, part, side, far, mix
        self.send, self.recv = send, recv
        self.rows = part.shape[0] // 4
        self.step = self.rows // CHUNKS

    def away(self, i):
        src = self.part.at[pl.ds(3 * self.rows + i * self.step, self.step)]
        dst = self.side.at[pl.ds(self.rows + i * self.step, self.step)]
        return remote(src, dst, self.send.at[0, i], self.recv.at[0, i], self.at["core"])

    def home(self, i):
        src = self.part.at[pl.ds(self.rows + i * self.step, self.step)]
        dst = self.side.at[pl.ds(i * self.step, self.step)]
        return remote(src, dst, self.send.at[1, i], self.recv.at[1, i], self.at["core"])

    def over(self, i):
        here = pl.ds(i * self.step, self.step)
        return remote(self.mix.at[here], self.far.at[here], self.send.at[2, i], self.recv.at[2, i], self.at["near"])

    def send_away(self):
        for i in range(CHUNKS):
            self.away(i).start()

    def send_home(self):
        for i in range(CHUNKS):
            self.home(i).start()

    def send_over(self):
        for i in range(CHUNKS):
            self.away(i).wait_recv()
            here = pl.ds(i * self.step, self.step)
            ours = self.part[pl.ds(2 * self.rows + i * self.step, self.step)].astype(F32)
            theirs = self.side[pl.ds(self.rows + i * self.step, self.step)].astype(F32)
            self.mix[here] = (ours + theirs).astype(BF16)
            self.over(i).start()

    def begin(self):
        self.send_away()
        self.send_home()
        self.send_over()

    def take(self, i):
        self.home(i).wait_recv()
        self.over(i).wait_recv()
        here = pl.ds(i * self.step, self.step)
        return self.part[here].astype(F32) + self.side[here].astype(F32) + self.far[here].astype(F32)

    def finish(self):
        for i in range(CHUNKS):
            self.away(i).wait_send()
            self.home(i).wait_send()
            self.over(i).wait_send()


def sems(*shape):
    return [pltpu.SemaphoreType.DMA(shape), pltpu.SemaphoreType.DMA(shape)]


def comm_params(number, mib=56):
    return pltpu.CompilerParams(collective_id=number, has_side_effects=True, vmem_limit_bytes=mib << 20)


VMEM_SPEC = pl.BlockSpec(memory_space=pltpu.VMEM)
ANY_SPEC = pl.BlockSpec(memory_space=pl.ANY)


def turn_kernel(part, cot, mid, gain, full, grad, side, far, mix, rs, rr, gs, gr):
    at = places()
    greet((at["core"], at["near"]))
    step = cot.shape[0] // CHUNKS
    total = Gathered(at, part, side, far, mix, rs, rr)
    spread = Spread(at, full, gs, gr)
    total.begin()
    for i in range(CHUNKS):
        here = slice(i * step, (i + 1) * step)
        unit, inverse = unit_rows(mid[here])
        value = cot[here].astype(F32) + unit_back(total.take(i), unit, inverse, gain[...])
        grad[here] = value
        full[here] = value.astype(BF16)
        spread.post(i)
    for i in range(CHUNKS):
        spread.forward(i)
    total.finish()
    spread.finish()


def turn_rows(part, cot, mid, gain):
    rows, width = cot.shape
    return pl.pallas_call(
        turn_kernel,
        in_specs=[VMEM_SPEC] * 4,
        out_specs=[VMEM_SPEC] * 2,
        out_shape=[jax.ShapeDtypeStruct((4 * rows, width), BF16), jax.ShapeDtypeStruct((rows, width), F32)],
        scratch_shapes=[VM((2 * rows, width), BF16), VM((rows, width), BF16), VM((rows, width), BF16)]
        + sems(3, CHUNKS) + sems(3, CHUNKS),
        compiler_params=comm_params(3, 40),
        name="turn_rows",
    )(part, cot, mid, gain)


def leave_kernel(part, tok, grad, gain, out, side, far, mix, done, rs, rr, os, orr):
    at = places()
    moved = at["moved"]
    greet((at["core"], at["near"]), (at["cross"],), moved)
    step = tok.shape[0] // CHUNKS
    total = Gathered(at, part, side, far, mix, rs, rr)

    def back(i):
        here = pl.ds(i * step, step)
        return remote(done.at[here], out.at[here], os.at[i], orr.at[i], at["cross"])

    total.begin()
    for i in range(CHUNKS):
        here = slice(i * step, (i + 1) * step)
        unit, inverse = unit_rows(tok[here].astype(F32))
        value = (grad[here] + unit_back(total.take(i), unit, inverse, gain[...])).astype(BF16)

        @pl.when(moved)
        def _():
            done[here] = value
            back(i).start()

        @pl.when(jnp.logical_not(moved))
        def _():
            out[here] = value

    total.finish()

    @pl.when(moved)
    def _():
        for i in range(CHUNKS):
            back(i).wait()


def leave(part, tok, grad, gain):
    rows, width = tok.shape
    return pl.pallas_call(
        leave_kernel,
        in_specs=[VMEM_SPEC] * 4,
        out_specs=VMEM_SPEC,
        out_shape=jax.ShapeDtypeStruct((rows, width), BF16),
        scratch_shapes=[
            VM((2 * rows, width), BF16), VM((rows, width), BF16), VM((rows, width), BF16), VM((rows, width), BF16)
        ] + sems(3, CHUNKS) + sems(CHUNKS),
        compiler_params=comm_params(4, 40),
        name="leave",
    )(part, tok, grad, gain)


class Supply:
    def __init__(self, at, plan, cross_send, cross_recv, share_send, share_recv):
        self.at, self.plan = at, plan
        self.xs, self.xr, self.ss, self.sr = cross_send, cross_recv, share_send, share_recv
        self.moved = at["moved"]
        self.peers = (at["left"], at["up"], at["both"])
        self.items = []
        for k, (native, role, shared, span) in enumerate(plan):
            size = native.shape[0] // 4 if shared else native.shape[0]
            for i in range(size // span):
                self.items.append((k, size, i))

    def rows(self, n):
        k, size, i = self.items[n]
        span = self.plan[k][3]
        if self.plan[k][2]:
            return pl.ds(pl.multiple_of(self.at["line"] * size + i * span, span), span)
        return pl.ds(i * span, span)

    def cross(self, n):
        native, role = self.plan[self.items[n][0]][:2]
        return remote(native.at[self.rows(n)], role.at[self.rows(n)], self.xs.at[n], self.xr.at[n], self.at["cross"])

    def share(self, n, k):
        role = self.plan[self.items[n][0]][1]
        block = role.at[self.rows(n)]
        return remote(block, block, self.ss.at[n, k], self.sr.at[n, k], self.peers[k])

    def begin(self, ahead):
        for n in range(ahead):
            self.cross(n).start()
        self.ahead = ahead

    def tick(self, n):
        @pl.when(self.moved)
        def _():
            self.cross(n).wait_recv()
            if n + self.ahead < len(self.items):
                self.cross(n + self.ahead).start()
            if self.plan[self.items[n][0]][2]:
                for k in range(3):
                    self.share(n, k).start()

    def ready(self, k):
        @pl.when(self.moved)
        def _():
            for n, item in enumerate(self.items):
                if item[0] == k:
                    for j in range(3):
                        self.share(n, j).wait_recv()

    def finish(self):
        @pl.when(self.moved)
        def _():
            for n, item in enumerate(self.items):
                self.cross(n).wait_send()
                if self.plan[item[0]][2]:
                    for j in range(3):
                        self.share(n, j).wait_send()


class Relay:
    def __init__(self, at, full, send, recv):
        self.at, self.full, self.send, self.recv = at, full, send, recv
        self.rows = full.shape[0] // 4

    def block(self, k, i):
        return self.full.at[pl.ds(k * self.rows + i * ITEM, ITEM)]

    def side(self, i):
        return remote(self.block(0, i), self.block(1, i), self.send.at[0, i], self.recv.at[0, i], self.at["core"])

    def far(self, i):
        return remote(self.block(0, i), self.block(2, i), self.send.at[1, i], self.recv.at[1, i], self.at["near"])

    def last(self, i):
        return remote(self.block(2, i), self.block(3, i), self.send.at[2, i], self.recv.at[2, i], self.at["core"])

    def post(self, i):
        self.far(i).start()
        self.side(i).start()

    def forward(self, i):
        self.far(i).wait_recv()
        self.last(i).start()

    def finish(self, count):
        for i in range(count):
            self.side(i).wait()
            self.far(i).wait_send()
            self.last(i).wait()


def pick_row(table, key):
    total = jnp.zeros(table.shape[1:], F32)
    for e in range(table.shape[0]):
        total = total + jnp.where(key == float(e), table[e].astype(F32), 0.0)
    return total.astype(BF16)


def front_kernel(
    ids, tokens, numbers, t_bq, t_ao, t_bu, t_ad, t_aq, t_bo, t_au, t_bd, norm_gains, norm_shifts, obias,
    w3, wo, wu, wd, cot,
    x, tok, small, nums, chosen, proj, lse, ctx, rank_qkv, rank_out, full, mid, cot_full, wqkv, wo_role, wu_role, wd_role,
    small_own, part, wv, wov, dist, vt, side, far, mix,
    ts, tr, ps, pr, xs, xr, ss, sr, cs, cr, rs, rr, gs, gr, load,
):
    at = places()
    moved = at["moved"]
    still = jnp.logical_not(moved)
    rows = tok.shape[0]
    step = rows // CHUNKS
    cols = wov.shape[0]
    rank = small.shape[0]
    greet((at["core"], at["near"]), (at["cross"], at["left"], at["up"], at["both"]), moved)
    qkv_span = w3.shape[1] // 4
    supply = Supply(
        at,
        [(w3.at[j], wqkv.at[j], True, qkv_span) for j in range(3)]
        + [(wo, wo_role, True, ITEM), (cot, cot_full, False, ITEM), (wu, wu_role, True, ITEM), (wd, wd_role, True, ITEM)],
        xs, xr, ss, sr,
    )
    relay = Relay(at, cot_full, cs, cr)

    def token(i):
        here = pl.ds(i * step, step)
        return remote(tokens.at[here], tok.at[here], ts.at[i], tr.at[i], at["cross"])

    def packs():
        return (
            remote(small_own, small, ps.at[0], pr.at[0], at["cross"]),
            remote(numbers, nums, ps.at[1], pr.at[1], at["cross"]),
        )

    @pl.when(moved)
    def _():
        for i in range(CHUNKS):
            token(i).start()
        supply.begin(AHEAD)

    for j in range(3):
        small_own[:, j * cols : (j + 1) * cols] = t_bq[ids[0], j]
    at_col = 3 * cols
    small_own[:, at_col : at_col + cols] = t_ao[ids[1]]
    at_col += cols
    wide = t_bu.shape[2]
    small_own[:, at_col : at_col + wide] = t_bu[ids[2]]
    at_col += wide
    small_own[:, at_col : at_col + wide] = t_ad[ids[3]]
    get_c = pltpu.make_async_copy(cot, cot_full.at[pl.ds(0, rows)], load.at[4])

    @pl.when(moved)
    def _():
        for copy in packs():
            copy.start()

    @pl.when(still)
    def _():
        get_c.start()
        tok[...] = tokens[...]
        small[...] = small_own[...]
        nums[...] = numbers[...]

    spread = Spread(at, x, gs.at[0], gr.at[0])
    for i in range(CHUNKS):
        here = slice(i * step, (i + 1) * step)

        @pl.when(moved)
        def _():
            token(i).wait_recv()

        unit, _ = unit_rows(tok[here].astype(F32))
        x[here] = (unit * norm_gains[0:1] + norm_shifts[0:1]).astype(BF16)
        spread.post(i)
    supply.tick(0)

    @pl.when(moved)
    def _():
        for copy in packs():
            copy.wait_recv()

    base = 2 * cols + wide
    key = lambda k: nums[0:1, base + k : base + k + 1]
    for k, table in enumerate((t_aq, t_bo, t_au, t_bd)):
        chosen[k * rank : (k + 1) * rank] = pick_row(table, key(2 + k))
    for i in range(CHUNKS):
        spread.forward(i)
    supply.tick(1)
    spread.finish()
    supply.tick(2)
    aq, bo = chosen[0:rank], chosen[rank : 2 * rank]
    rank_qkv[...] = dot_t(x[...], aq).astype(BF16)
    for j in range(3):
        supply.ready(j)
        fetch(w3.at[j], wqkv.at[j], wv.at[j], load.at[j]).wait()
        span = slice(j * cols, (j + 1) * cols)

        def strip(i, carry):
            here = pl.ds(pl.multiple_of(i * rows, rows), rows)
            value = dot(x[here], wv[j]) + dot(rank_qkv[here], small[:, span])
            if j != 1:
                value = value + nums[0:1, (j // 2) * cols : (j // 2 + 1) * cols]
            proj[here, span] = value.astype(BF16)
            return carry

        lax.fori_loop(0, 4, strip, 0)
    supply.tick(3)
    me = 2 * (lax.axis_index("dp") % 2) + lax.axis_index("tensor") % 2
    vt[...] = proj[:, 2 * cols :].T
    scale = LOG2E / math.sqrt(HEAD_DIM)
    slopes = head_slopes(me, cols // HEAD_DIM)

    def attend_step(i, carry):
        here = pl.ds(pl.multiple_of(i * rows, rows), rows)
        distances(me, key(0), key(1), rows, i, dist)
        for h in range(cols // HEAD_DIM):
            span = slice(h * HEAD_DIM, (h + 1) * HEAD_DIM)
            keys = proj[:, cols + h * HEAD_DIM : cols + (h + 1) * HEAD_DIM]
            s = dot_t(keys, proj[here, span]) * scale - dist[...] * slopes[h]
            peak = jnp.max(s, axis=0, keepdims=True)
            e = jnp.exp2(s - peak)
            total = jnp.sum(e, axis=0, keepdims=True)
            c = dot(vt[span, :], e.astype(BF16)) * (1.0 / total)
            ctx[here, span] = c.T.astype(BF16)
            lse[h : h + 1, here] = peak + jnp.log2(total)
        return carry

    def attend(first, count):
        lax.fori_loop(first, first + count, attend_step, 0)

    attend(0, 1)
    supply.tick(4)

    @pl.when(still)
    def _():
        get_c.wait()

    relay.post(0)
    attend(1, 1)
    supply.tick(5)
    relay.post(1)
    attend(2, 1)
    supply.tick(6)
    relay.forward(0)
    attend(3, 1)
    supply.tick(7)
    relay.forward(1)
    supply.ready(3)
    fetch(wo, wo_role, wov, load.at[3]).wait()
    ao = small[:, 3 * cols : 4 * cols]

    def out_rows(i):
        here = pl.ds(i * rows, rows)
        r = dot_t(ctx[here], ao).astype(BF16)
        rank_out[here] = r
        part[here] = (dot(ctx[here], wov[...]) + dot(r, bo)).astype(BF16)

    total = Gathered(at, part, side, far, mix, rs, rr)
    out_rows(3)
    total.send_away()
    out_rows(1)
    total.send_home()
    out_rows(2)
    total.send_over()
    out_rows(0)
    supply.tick(8)
    spread_mid = Spread(at, full, gs.at[1], gr.at[1])
    for i in range(CHUNKS):
        here = slice(i * step, (i + 1) * step)
        value = tok[here].astype(F32) + (total.take(i) + obias[...])
        mid[here] = value
        unit, _ = unit_rows(value)
        full[here] = (unit * norm_gains[1:2] + norm_shifts[1:2]).astype(BF16)
        spread_mid.post(i)
        if i % 2 == 1:
            supply.tick(9 + i // 2)
    for i in range(CHUNKS):
        spread_mid.forward(i)
        if i == 1:
            supply.tick(11)
    for n in range(12, len(supply.items)):
        supply.tick(n)
    total.finish()
    spread_mid.finish()
    relay.finish(2)
    for k in (5, 6):
        supply.ready(k)
    supply.finish()

    @pl.when(moved)
    def _():
        for i in range(CHUNKS):
            token(i).wait_send()
        for copy in packs():
            copy.wait_send()


def front(ids, tokens, numbers, tables, norm_gains, norm_shifts, obias, w3, wo, wu, wd, cot):
    rows, width = tokens.shape
    n = 4 * rows
    cols = w3.shape[2]
    rank = tables[1].shape[1]
    packed = 4 * cols + 2 * wu.shape[1]
    items = 3 + (wo.shape[0] + wu.shape[0] + wd.shape[0]) // 4 // ITEM + rows // ITEM
    low = lambda *s: jax.ShapeDtypeStruct(s, BF16)
    high = lambda *s: jax.ShapeDtypeStruct(s, F32)
    return pl.pallas_call(
        front_kernel,
        in_specs=[pl.BlockSpec(memory_space=pltpu.SMEM)] + [VMEM_SPEC] * 13 + [ANY_SPEC] * 5,
        out_specs=[VMEM_SPEC] * 12 + [ANY_SPEC] * 5,
        out_shape=[
            low(n, width), low(rows, width), low(rank, packed), high(*numbers.shape), low(4 * rank, width),
            low(n, 3 * cols), high(cols // HEAD_DIM, n), low(n, cols), low(n, rank), low(n, rank),
            low(n, width), high(rows, width), low(n, width), low(*w3.shape), low(*wo.shape), low(*wu.shape), low(*wd.shape),
        ],
        scratch_shapes=[
            VM((rank, packed), BF16),
            VM((n, width), BF16), VM(w3.shape, BF16), VM(wo.shape, BF16), VM((n, rows), F32), VM((cols, n), BF16),
            VM((2 * rows, width), BF16), VM((rows, width), BF16), VM((rows, width), BF16),
        ]
        + sems(CHUNKS) + sems(2) + sems(items) + sems(items, 3) + sems(3, rows // ITEM)
        + sems(3, CHUNKS) + sems(2, 3, CHUNKS) + [pltpu.SemaphoreType.DMA((5,))],
        compiler_params=comm_params(1, 60),
        name="front",
    )(ids, tokens, numbers, *tables, norm_gains, norm_shifts, obias, w3, wo, wu, wd, cot)


def routes(nd, nt):
    def lin(d, t):
        return d * nt + t

    every = [(d, t) for d in range(nd) for t in range(nt)]
    moved = [(d, t) for d, t in every if (d & 1) != (t >> 1)]
    both = [(lin(d, t), lin(d ^ 1, t ^ 2)) for d, t in moved]
    return dict(
        swap=both + [(lin(d, t), lin(d, t)) for d, t in every if (d & 1) == (t >> 1)],
        cross=both,
        core=[(lin(d, t), lin(d ^ 1, t)) for d, t in every],
        near=[(lin(d, t), lin(d, t ^ 1)) for d, t in every],
        left=[(lin(d, t), lin(d ^ 2, t)) for d, t in moved],
        up=[(lin(d, t), lin(d ^ 4, t)) for d, t in moved],
    )


def body(
    tokens, cotangent, norm_gains, norm_shifts, query_key_value_weight, b_qv, output_weight,
    output_bias_vector, up_weight, b_up, down_weight, down_bias_vector, adapter_query_key_value_input,
    qkv_out, adapter_output_input, adapter_output_output, adapter_up_input, up_out, down_in,
    adapter_down_output, offsets, adapter_ids,
):
    nd, nt = lax.axis_size("dp"), lax.axis_size("tensor")
    route = routes(nd, nt)
    d, t = lax.axis_index("dp"), lax.axis_index("tensor")
    c, p = d % 2, (d // 2) % 4
    moved = c != t // 2
    me = 2 * c + t % 2
    rows, width = tokens.shape
    length = rows * nt
    local = output_weight.shape[0]
    local_heads = local // HEAD_DIM
    hidden_width = up_weight.shape[1]
    rank = adapter_up_input.shape[1]
    tables = adapter_up_input.shape[0]

    def go(x, name):
        return lax.ppermute(x, AXES, route[name])

    w3 = jnp.transpose(query_key_value_weight, (1, 0, 2))
    b3 = jnp.transpose(qkv_out, (0, 2, 1, 3))
    extra = jnp.pad(jnp.concatenate([offsets, adapter_ids], 1).astype(F32), ((0, 0), (0, 122)))
    numbers = jnp.concatenate([b_qv.reshape(1, 2 * local), b_up.reshape(1, hidden_width), extra], 1)
    tables_in = (
        b3, adapter_output_input, up_out, down_in, adapter_query_key_value_input, adapter_output_output,
        adapter_up_input, adapter_down_output,
    )
    (
        x, tok, small, nums, chosen, proj, lse, ctx, rank_qkv, rank_out, nm, middle, cot, wqkv, wo, wu, wd,
    ) = front(
        adapter_ids[0], tokens, numbers, tables_in, norm_gains, norm_shifts, output_bias_vector.reshape(1, width),
        w3, output_weight, up_weight, down_weight, cotangent,
    )
    cuts = [3 * local, 4 * local, 4 * local + hidden_width]
    gain = [norm_gains[i : i + 1] for i in range(2)]

    def scatter(home, away):
        far = (away[:rows].astype(F32) + go(away[rows:], "core").astype(F32)).astype(BF16)
        far = go(far, "near")
        side = go(home[rows:], "core")
        return home[:rows].astype(F32) + side.astype(F32) + far.astype(F32)

    part, back, t_up_out, t_down_in, t_up_in, t_down_out = mlp(
        nm, cot, up_weight, wu, down_weight, wd, chosen, small, nums, hidden_width // 4
    )
    cot_own = cot[:rows]
    gm, grad_middle = turn_rows(back, cot_own, middle, gain[1])
    result = (middle + (scatter(part[: 2 * rows], part[2 * rows :]) + down_bias_vector)).astype(BF16)
    grad_ctx, t_out_out, t_out_in = bwd_o(gm, output_weight, wo, chosen, small, rank_out, ctx, rows)
    grad_proj = attend_back(nums, proj, grad_ctx, lse, rows)
    gx, t_qkv_out, t_qkv_in = bwd_qkv(grad_proj, w3, wqkv, small, chosen, rank_qkv, x, rows)
    in_grad = leave(gx, tok, grad_middle, gain[0])

    result = go(result, "swap")

    def owned(pieces):
        return lax.all_gather(go(jnp.concatenate(pieces, 1).astype(BF16), "swap"), "dp", axis=0)

    everyone = lax.all_gather(adapter_ids, "dp", axis=0, tiled=True)
    hot = (everyone[:, :, None] == jnp.arange(tables, dtype=jnp.int32)).astype(BF16)

    def combine(per, which):
        return jnp.einsum("se,srm->erm", hot[:, which], per, preferred_element_type=F32)

    own = owned([t[:rank] for t in (t_qkv_out, t_out_in, t_up_out, t_down_in)])
    g_qkv_out = jnp.einsum(
        "se,srkm->erkm", hot[:, 0], own[:, :, : cuts[0]].reshape(nd, rank, 3, local), preferred_element_type=F32
    )
    g_out_in = combine(own[:, :, cuts[0] : cuts[1]], 1)
    g_up_out = combine(own[:, :, cuts[1] : cuts[2]], 2)
    g_down_in = combine(own[:, :, cuts[2] :], 3)

    shared = jnp.stack([t[:rank] for t in (t_qkv_in, t_out_out, t_up_in, t_down_out)]).astype(BF16)
    shared = shared.astype(F32) + go(shared, "core").astype(F32)
    shared = (shared + go(shared.astype(BF16), "near").astype(F32)).astype(BF16)
    quarter = width // 4
    mine = lax.dynamic_slice_in_dim(shared, me * quarter, quarter, 2)
    mine = go(mine, "swap")
    mine = lax.all_gather(mine, "dp", axis=0)
    sums = jnp.einsum("ske,skrm->kerm", hot.transpose(0, 1, 2), mine, preferred_element_type=F32)
    whole = lax.all_gather(sums.astype(BF16), "tensor", axis=3, tiled=True).astype(F32)
    return (
        result, in_grad, whole[0], g_qkv_out, g_out_in, whole[1], whole[2], g_up_out, g_down_in, whole[3],
    )


def solution(mesh):
    placed = (
        P(("dp", "tensor"), None), P(("dp", "tensor"), None), P(), P(), P(None, None, "tensor"), P(None, "tensor"),
        P("tensor", None), P(), P(None, "tensor"), P("tensor"), P("tensor", None), P(), P(),
        P(None, None, None, "tensor"), P(None, None, "tensor"), P(), P(), P(None, None, "tensor"),
        P(None, None, "tensor"), P(), P("dp", None), P("dp", None),
    )
    return jax.shard_map(
        body, mesh=mesh, in_specs=placed,
        out_specs=(
            P(("dp", "tensor"), None), P(("dp", "tensor"), None), P(), P(None, None, None, "tensor"),
            P(None, None, "tensor"), P(), P(), P(None, None, "tensor"), P(None, None, "tensor"), P(),
        ),
        check_vma=False,
    )
```

```python
import functools
import math

import jax
import jax.numpy as jnp
from jax import lax
from jax.experimental import pallas as pl
from jax.experimental.pallas import tpu as pltpu
from jax.sharding import PartitionSpec as P

HEADS = 16
HEAD_DIM = 128
PIECE = 256
ITEM = 128
AHEAD = 2
EPS = 1e-05
GELU_C = 0.7978845608028654
GELU_K = 0.044715
LOG2E = 1.4426950408889634
FAR = 1e32
F32 = jnp.float32
BF16 = jnp.bfloat16
AXES = ("dp", "tensor")
VM = pltpu.VMEM
HERE = pl.BlockSpec(memory_space=pl.ANY)


def dot(a, b):
    return lax.dot_general(a, b, (((1,), (0,)), ((), ())), preferred_element_type=F32)


def dot_t(a, b):
    return lax.dot_general(a, b, (((1,), (1,)), ((), ())), preferred_element_type=F32)


def t_dot(a, b):
    return lax.dot_general(a, b, (((0,), (0,)), ((), ())), preferred_element_type=F32)


def whole(shape):
    zeros = (0,) * len(shape)
    return pl.BlockSpec(shape, lambda *_: zeros)


def params(mib=56):
    return pltpu.CompilerParams(vmem_limit_bytes=mib << 20)


def cost(flops, read):
    return pl.CostEstimate(flops=int(flops), bytes_accessed=int(read), transcendentals=0)


def displaced():
    return (lax.axis_index("dp") % 2 + lax.axis_index("tensor") // 2) % 2 == 1


def fetch(native, brought, into, sem):
    moved = displaced()

    @pl.when(moved)
    def _():
        pltpu.make_async_copy(brought, into, sem).start()

    @pl.when(jnp.logical_not(moved))
    def _():
        pltpu.make_async_copy(native, into, sem).start()

    return pltpu.make_async_copy(native, into, sem)


def distances(me, s0, s1, rows, step, dist):
    length = dist.shape[0]

    def piece(pos, none):
        one = jnp.where((pos >= s0) & (pos < s0 + PIECE), 1.0, none)
        return jnp.where((pos >= s1) & (pos < s1 + PIECE), 2.0, one)

    def rel(j):
        return ((j & 1) << 1) | (j >> 1)

    i = lax.broadcasted_iota(jnp.int32, (length, 128), 0)
    kpos = ((me ^ rel(i // rows)) * rows + i % rows).astype(F32)[:, :1]
    qpos = ((me ^ rel(step)) * rows + lax.broadcasted_iota(jnp.int32, (1, rows), 1)).astype(F32)
    seen = (kpos <= qpos) | (piece(kpos, -1.0) == piece(qpos, -2.0))
    dist[...] = jnp.where(seen, jnp.abs(kpos - qpos), FAR)


def head_slopes(me, heads):
    first = jnp.full((1, 1), me * heads, jnp.int32).astype(F32)
    return [jnp.exp2((first + float(h + 1)) * (-8.0 / HEADS)) * LOG2E for h in range(heads)]


def gelu_parts(values):
    square = values * values
    tangent = jnp.tanh(GELU_C * (values + GELU_K * square * values))
    half = 0.5 * (1.0 + tangent)
    slope = half + (0.5 * GELU_C) * values * (1.0 - tangent * tangent) * (1.0 + 3.0 * GELU_K * square)
    return values * half, slope


def mlp_kernel(
    nm, cot, wu_native, wu_brought, wd_native, wd_brought, au, bu, ad, bd, bias, part, back, tuo, tdi, tui, tdo,
    up_rank, down_rank, g_up, g_down, acc, gacc, wu_slots, wd_slots, sem,
):
    step, half = pl.program_id(0), pl.program_id(1)
    last = pl.num_programs(0) - 1
    rows = nm.shape[0]
    tile = bu.shape[1]

    def load(j):
        slot = j % 2
        cut = pl.ds(pl.multiple_of(j * tile, tile), tile)
        return (
            fetch(wu_native.at[:, cut], wu_brought.at[:, cut], wu_slots.at[slot], sem.at[0, slot]),
            fetch(wd_native.at[cut], wd_brought.at[cut], wd_slots.at[slot], sem.at[1, slot]),
        )

    def await_slot(slot):
        pltpu.make_async_copy(wu_native.at[:, pl.ds(0, tile)], wu_slots.at[slot], sem.at[0, slot]).wait()
        pltpu.make_async_copy(wd_native.at[pl.ds(0, tile)], wd_slots.at[slot], sem.at[1, slot]).wait()

    @pl.when((step == 0) & (half == 0))
    def _():
        load(step)

    @pl.when(half == 0)
    def _():
        await_slot(step % 2)

        @pl.when(step < last)
        def _():
            load(step + 1)

    wu = wu_slots.at[step % 2]
    wd = wd_slots.at[step % 2]
    here = pl.ds(pl.multiple_of(half * rows, rows), rows)

    @pl.when(step == 0)
    def _():
        up_rank[here] = dot_t(nm[...], au[...]).astype(BF16)
        g_down[here] = dot_t(cot[...], bd[...]).astype(BF16)
        down_rank[here] = jnp.zeros((rows, au.shape[0]), F32)
        g_up[here] = jnp.zeros((rows, au.shape[0]), F32)
        acc[here] = jnp.zeros((rows, nm.shape[1]), F32)
        gacc[here] = jnp.zeros((rows, nm.shape[1]), F32)

    gate = dot(nm[...], wu[...]) + dot(up_rank[here], bu[...]) + bias[...]
    value, slope = gelu_parts(gate)
    hidden = value.astype(BF16)
    grad = dot_t(cot[...], wd[...]) + dot(g_down[here], ad[...])
    grad_gate = (grad * slope).astype(BF16)
    down_rank[here] += dot_t(hidden, ad[...])
    g_up[here] += dot_t(grad_gate, bu[...])
    acc[here] += dot(hidden, wd[...])
    gacc[here] += dot_t(grad_gate, wu[...])
    one = t_dot(up_rank[here], grad_gate)
    two = t_dot(g_down[here], hidden)

    @pl.when(half == 0)
    def _():
        tuo[...] = one
        tdi[...] = two

    @pl.when(half > 0)
    def _():
        tuo[...] += one
        tdi[...] += two

    @pl.when(step == last)
    def _():
        dr = down_rank[here].astype(BF16)
        gu = g_up[here].astype(BF16)
        part[...] = (acc[here] + dot(dr, bd[...])).astype(BF16)
        back[...] = (gacc[here] + dot(gu, au[...])).astype(BF16)
        three = t_dot(gu, nm[...])
        four = t_dot(dr, cot[...])

        @pl.when(half == 0)
        def _():
            tui[...] = three
            tdo[...] = four

        @pl.when(half > 0)
        def _():
            tui[...] += three
            tdo[...] += four


def mlp(nm, cot, wu, wu_brought, wd, wd_brought, chosen, small, nums, tile):
    n, width = nm.shape
    rows = n // 2
    hidden = wu.shape[1]
    last = hidden // tile - 1
    low = small.shape[0]
    first = (small.shape[1] - 2 * hidden) // tile
    bias_first = (nums.shape[1] - 128 - hidden) // tile
    cut = lambda r: pl.BlockSpec((r, tile), lambda j, i: (0, j))
    row = pl.BlockSpec((rows, width), lambda j, i: (i, 0))
    result = pl.BlockSpec((rows, width), lambda j, i: (jnp.where(j == last, i, 0), 0))
    return pl.pallas_call(
        mlp_kernel,
        grid=(hidden // tile, 2),
        in_specs=[
            row, row, HERE, HERE, HERE, HERE,
            pl.BlockSpec((low, width), lambda j, i: (2, 0)),
            pl.BlockSpec((low, tile), lambda j, i: (0, first + j)),
            pl.BlockSpec((low, tile), lambda j, i: (0, first + hidden // tile + j)),
            pl.BlockSpec((low, width), lambda j, i: (3, 0)),
            pl.BlockSpec((1, tile), lambda j, i: (0, bias_first + j)),
        ],
        out_specs=[result, result, cut(low), cut(low), whole((low, width)), whole((low, width))],
        out_shape=[
            jax.ShapeDtypeStruct((n, width), BF16),
            jax.ShapeDtypeStruct((n, width), BF16),
            jax.ShapeDtypeStruct((low, hidden), F32),
            jax.ShapeDtypeStruct((low, hidden), F32),
            jax.ShapeDtypeStruct((low, width), F32),
            jax.ShapeDtypeStruct((low, width), F32),
        ],
        scratch_shapes=[
            VM((n, low), BF16), VM((n, low), F32), VM((n, low), F32), VM((n, low), BF16),
            VM((n, width), F32), VM((n, width), F32),
            VM((2, width, tile), BF16), VM((2, tile, width), BF16), pltpu.SemaphoreType.DMA((2, 2)),
        ],
        compiler_params=params(60),
        cost_estimate=cost(8 * n * width * hidden, 4 * width * hidden + 12 * n * width),
        name="mlp",
    )(nm, cot, wu, wu_brought, wd, wd_brought, chosen, small, small, chosen, nums)


MESH = pl.DeviceIdType.MESH
CHUNKS = 4


def places():
    d, t = lax.axis_index("dp"), lax.axis_index("tensor")
    core, zh = d % 2, t // 2
    core_d = d + 1 - 2 * core
    near_t = t + 1 - 2 * (t % 2)
    left = d + 2 - 4 * ((d // 2) % 2)
    up = 4 - 8 * ((d // 4) % 2)
    return dict(
        moved=(core + zh) % 2 == 1,
        line=(d // 2) % 4,
        core=(core_d, t),
        near=(d, near_t),
        cross=(core_d, t + 2 - 4 * zh),
        left=(left, t),
        up=(d + up, t),
        both=(left + up, t),
    )


def greet(always, sometimes=(), when=None):
    barrier = pltpu.get_barrier_semaphore()
    for peer in always:
        pl.semaphore_signal(barrier, inc=1, device_id=peer, device_id_type=MESH)
    count = len(always)
    if sometimes:

        @pl.when(when)
        def _():
            for peer in sometimes:
                pl.semaphore_signal(barrier, inc=1, device_id=peer, device_id_type=MESH)

        count = count + len(sometimes) * when.astype(jnp.int32)
    pl.semaphore_wait(barrier, count)


def remote(src, dst, send, recv, peer):
    return pltpu.make_async_remote_copy(
        src_ref=src, dst_ref=dst, send_sem=send, recv_sem=recv, device_id=peer, device_id_type=MESH
    )


def unit_rows(v):
    centre = v - jnp.mean(v, axis=-1, keepdims=True)
    inverse = lax.rsqrt(jnp.mean(centre * centre, axis=-1, keepdims=True) + EPS)
    return centre * inverse, inverse


def unit_back(grad, scaled, inverse, gain):
    inner = grad * gain
    first = jnp.mean(inner, axis=-1, keepdims=True)
    second = jnp.mean(inner * scaled, axis=-1, keepdims=True)
    return inverse * (inner - first - scaled * second)


class Spread:
    def __init__(self, at, full, send, recv):
        self.at, self.full, self.send, self.recv = at, full, send, recv
        self.rows = full.shape[0] // 4
        self.step = self.rows // CHUNKS

    def block(self, k, i):
        return self.full.at[pl.ds(k * self.rows + i * self.step, self.step)]

    def side(self, i):
        return remote(self.block(0, i), self.block(1, i), self.send.at[0, i], self.recv.at[0, i], self.at["core"])

    def far(self, i):
        return remote(self.block(0, i), self.block(2, i), self.send.at[1, i], self.recv.at[1, i], self.at["near"])

    def onward(self, i):
        return remote(self.block(2, i), self.block(3, i), self.send.at[2, i], self.recv.at[2, i], self.at["core"])

    def post(self, i):
        self.far(i).start()
        self.side(i).start()

    def forward(self, i):
        self.far(i).wait_recv()
        self.onward(i).start()

    def finish(self):
        for i in range(CHUNKS):
            self.side(i).wait()
            self.far(i).wait_send()
            self.onward(i).wait()


class Gathered:
    def __init__(self, at, part, side, far, mix, send, recv, kept=None):
        self.at, self.part, self.side, self.far, self.mix = at, part, side, far, mix
        self.kept, self.second = (part, 2) if kept is None else (kept, 1)
        self.send, self.recv = send, recv
        self.rows = part.shape[0] // 4
        self.step = self.rows // CHUNKS

    def away(self, i):
        src = self.part.at[pl.ds(3 * self.rows + i * self.step, self.step)]
        dst = self.side.at[pl.ds(self.rows + i * self.step, self.step)]
        return remote(src, dst, self.send.at[0, i], self.recv.at[0, i], self.at["core"])

    def home(self, i):
        src = self.part.at[pl.ds(self.rows + i * self.step, self.step)]
        dst = self.side.at[pl.ds(i * self.step, self.step)]
        return remote(src, dst, self.send.at[1, i], self.recv.at[1, i], self.at["core"])

    def over(self, i):
        here = pl.ds(i * self.step, self.step)
        return remote(self.mix.at[here], self.far.at[here], self.send.at[2, i], self.recv.at[2, i], self.at["near"])

    def send_away(self):
        for i in range(CHUNKS):
            self.away(i).start()

    def send_home(self):
        for i in range(CHUNKS):
            self.home(i).start()

    def send_over(self):
        for i in range(CHUNKS):
            self.away(i).wait_recv()
            here = pl.ds(i * self.step, self.step)
            ours = self.kept[pl.ds(self.second * self.rows + i * self.step, self.step)].astype(F32)
            theirs = self.side[pl.ds(self.rows + i * self.step, self.step)].astype(F32)
            self.mix[here] = (ours + theirs).astype(BF16)
            self.over(i).start()

    def begin(self):
        self.send_away()
        self.send_home()
        self.send_over()

    def take(self, i):
        self.home(i).wait_recv()
        self.over(i).wait_recv()
        here = pl.ds(i * self.step, self.step)
        return self.kept[here].astype(F32) + self.side[here].astype(F32) + self.far[here].astype(F32)

    def finish(self):
        for i in range(CHUNKS):
            self.away(i).wait_send()
            self.home(i).wait_send()
            self.over(i).wait_send()


def sems(*shape):
    return [pltpu.SemaphoreType.DMA(shape), pltpu.SemaphoreType.DMA(shape)]


def comm_params(number, mib=56):
    return pltpu.CompilerParams(collective_id=number, has_side_effects=True, vmem_limit_bytes=mib << 20)


VMEM_SPEC = pl.BlockSpec(memory_space=pltpu.VMEM)
ANY_SPEC = pl.BlockSpec(memory_space=pl.ANY)


class Supply:
    def __init__(self, at, plan, cross_send, cross_recv, share_send, share_recv):
        self.at, self.plan = at, plan
        self.xs, self.xr, self.ss, self.sr = cross_send, cross_recv, share_send, share_recv
        self.moved = at["moved"]
        self.peers = (at["left"], at["up"], at["both"])
        self.items = []
        for k, (native, role, shared, span) in enumerate(plan):
            size = native.shape[0] // 4 if shared else native.shape[0]
            for i in range(size // span):
                self.items.append((k, size, i))

    def rows(self, n):
        k, size, i = self.items[n]
        span = self.plan[k][3]
        if self.plan[k][2]:
            return pl.ds(pl.multiple_of(self.at["line"] * size + i * span, span), span)
        return pl.ds(i * span, span)

    def cross(self, n):
        native, role = self.plan[self.items[n][0]][:2]
        return remote(native.at[self.rows(n)], role.at[self.rows(n)], self.xs.at[n], self.xr.at[n], self.at["cross"])

    def share(self, n, k):
        role = self.plan[self.items[n][0]][1]
        block = role.at[self.rows(n)]
        return remote(block, block, self.ss.at[n, k], self.sr.at[n, k], self.peers[k])

    def begin(self, ahead):
        for n in range(ahead):
            self.cross(n).start()
        self.ahead = ahead

    def tick(self, n):
        @pl.when(self.moved)
        def _():
            self.cross(n).wait_recv()
            if n + self.ahead < len(self.items):
                self.cross(n + self.ahead).start()
            if self.plan[self.items[n][0]][2]:
                for k in range(3):
                    self.share(n, k).start()

    def ready(self, k):
        @pl.when(self.moved)
        def _():
            for n, item in enumerate(self.items):
                if item[0] == k:
                    for j in range(3):
                        self.share(n, j).wait_recv()

    def finish(self):
        @pl.when(self.moved)
        def _():
            for n, item in enumerate(self.items):
                self.cross(n).wait_send()
                if self.plan[item[0]][2]:
                    for j in range(3):
                        self.share(n, j).wait_send()


class Relay:
    def __init__(self, at, full, send, recv):
        self.at, self.full, self.send, self.recv = at, full, send, recv
        self.rows = full.shape[0] // 4

    def block(self, k, i):
        return self.full.at[pl.ds(k * self.rows + i * ITEM, ITEM)]

    def side(self, i):
        return remote(self.block(0, i), self.block(1, i), self.send.at[0, i], self.recv.at[0, i], self.at["core"])

    def far(self, i):
        return remote(self.block(0, i), self.block(2, i), self.send.at[1, i], self.recv.at[1, i], self.at["near"])

    def last(self, i):
        return remote(self.block(2, i), self.block(3, i), self.send.at[2, i], self.recv.at[2, i], self.at["core"])

    def post(self, i):
        self.far(i).start()
        self.side(i).start()

    def forward(self, i):
        self.far(i).wait_recv()
        self.last(i).start()

    def finish(self, count):
        for i in range(count):
            self.side(i).wait()
            self.far(i).wait_send()
            self.last(i).wait()


def pick_row(table, key):
    total = jnp.zeros(table.shape[1:], F32)
    for e in range(table.shape[0]):
        total = total + jnp.where(key == float(e), table[e].astype(F32), 0.0)
    return total.astype(BF16)


def front_kernel(
    ids, tokens, numbers, t_bq, t_ao, t_bu, t_ad, t_aq, t_bo, t_au, t_bd, norm_gains, norm_shifts, obias,
    w3, wo, wu, wd, cot,
    x, tok, small, nums, chosen, proj, lse, ctx, rank_qkv, rank_out, full, mid, cot_full, wqkv, wo_role, wu_role, wd_role,
    small_own, part, wv, wov, dist, vt, side, far, mix,
    ts, tr, ps, pr, xs, xr, ss, sr, cs, cr, rs, rr, gs, gr, load,
):
    at = places()
    moved = at["moved"]
    still = jnp.logical_not(moved)
    rows = tok.shape[0]
    step = rows // CHUNKS
    cols = wov.shape[0]
    rank = small.shape[0]
    greet((at["core"], at["near"]), (at["cross"], at["left"], at["up"], at["both"]), moved)
    qkv_span = w3.shape[1] // 4
    supply = Supply(
        at,
        [(w3.at[j], wqkv.at[j], True, qkv_span) for j in range(3)]
        + [(wo, wo_role, True, ITEM), (cot, cot_full, False, ITEM), (wu, wu_role, True, ITEM), (wd, wd_role, True, ITEM)],
        xs, xr, ss, sr,
    )
    relay = Relay(at, cot_full, cs, cr)

    def token(i):
        here = pl.ds(i * step, step)
        return remote(tokens.at[here], tok.at[here], ts.at[i], tr.at[i], at["cross"])

    def packs():
        return (
            remote(small_own, small, ps.at[0], pr.at[0], at["cross"]),
            remote(numbers, nums, ps.at[1], pr.at[1], at["cross"]),
        )

    @pl.when(moved)
    def _():
        for i in range(CHUNKS):
            token(i).start()
        supply.begin(AHEAD)

    for j in range(3):
        small_own[:, j * cols : (j + 1) * cols] = t_bq[ids[0], j]
    at_col = 3 * cols
    small_own[:, at_col : at_col + cols] = t_ao[ids[1]]
    at_col += cols
    wide = t_bu.shape[2]
    small_own[:, at_col : at_col + wide] = t_bu[ids[2]]
    at_col += wide
    small_own[:, at_col : at_col + wide] = t_ad[ids[3]]
    get_c = pltpu.make_async_copy(cot, cot_full.at[pl.ds(0, rows)], load.at[4])

    @pl.when(moved)
    def _():
        for copy in packs():
            copy.start()

    @pl.when(still)
    def _():
        get_c.start()
        tok[...] = tokens[...]
        small[...] = small_own[...]
        nums[...] = numbers[...]

    spread = Spread(at, x, gs.at[0], gr.at[0])
    for i in range(CHUNKS):
        here = slice(i * step, (i + 1) * step)

        @pl.when(moved)
        def _():
            token(i).wait_recv()

        unit, _ = unit_rows(tok[here].astype(F32))
        x[here] = (unit * norm_gains[0:1] + norm_shifts[0:1]).astype(BF16)
        spread.post(i)
    supply.tick(0)

    @pl.when(moved)
    def _():
        for copy in packs():
            copy.wait_recv()

    base = 2 * cols + wide
    key = lambda k: nums[0:1, base + k : base + k + 1]
    for k, table in enumerate((t_aq, t_bo, t_au, t_bd)):
        chosen[k * rank : (k + 1) * rank] = pick_row(table, key(2 + k))
    for i in range(CHUNKS):
        spread.forward(i)
    supply.tick(1)
    spread.finish()
    supply.tick(2)
    aq, bo = chosen[0:rank], chosen[rank : 2 * rank]
    rank_qkv[...] = dot_t(x[...], aq).astype(BF16)
    for j in range(3):
        supply.ready(j)
        fetch(w3.at[j], wqkv.at[j], wv.at[j], load.at[j]).wait()
        span = slice(j * cols, (j + 1) * cols)

        def strip(i, carry):
            here = pl.ds(pl.multiple_of(i * rows, rows), rows)
            value = dot(x[here], wv[j]) + dot(rank_qkv[here], small[:, span])
            if j != 1:
                value = value + nums[0:1, (j // 2) * cols : (j // 2 + 1) * cols]
            proj[here, span] = value.astype(BF16)
            return carry

        lax.fori_loop(0, 4, strip, 0)
    supply.tick(3)
    me = 2 * (lax.axis_index("dp") % 2) + lax.axis_index("tensor") % 2
    vt[...] = proj[:, 2 * cols :].T
    scale = LOG2E / math.sqrt(HEAD_DIM)
    slopes = head_slopes(me, cols // HEAD_DIM)

    def attend_step(i, carry):
        here = pl.ds(pl.multiple_of(i * rows, rows), rows)
        distances(me, key(0), key(1), rows, i, dist)
        for h in range(cols // HEAD_DIM):
            span = slice(h * HEAD_DIM, (h + 1) * HEAD_DIM)
            keys = proj[:, cols + h * HEAD_DIM : cols + (h + 1) * HEAD_DIM]
            s = dot_t(keys, proj[here, span]) * scale - dist[...] * slopes[h]
            peak = jnp.max(s, axis=0, keepdims=True)
            e = jnp.exp2(s - peak)
            total = jnp.sum(e, axis=0, keepdims=True)
            c = dot(vt[span, :], e.astype(BF16)) * (1.0 / total)
            ctx[here, span] = c.T.astype(BF16)
            lse[h : h + 1, here] = peak + jnp.log2(total)
        return carry

    def attend(first, count):
        lax.fori_loop(first, first + count, attend_step, 0)

    attend(0, 1)
    supply.tick(4)

    @pl.when(still)
    def _():
        get_c.wait()

    relay.post(0)
    attend(1, 1)
    supply.tick(5)
    relay.post(1)
    attend(2, 1)
    supply.tick(6)
    relay.forward(0)
    attend(3, 1)
    supply.tick(7)
    relay.forward(1)
    supply.ready(3)
    fetch(wo, wo_role, wov, load.at[3]).wait()
    ao = small[:, 3 * cols : 4 * cols]

    def out_rows(i):
        here = pl.ds(i * rows, rows)
        r = dot_t(ctx[here], ao).astype(BF16)
        rank_out[here] = r
        part[here] = (dot(ctx[here], wov[...]) + dot(r, bo)).astype(BF16)

    total = Gathered(at, part, side, far, mix, rs, rr)
    out_rows(3)
    total.send_away()
    out_rows(1)
    total.send_home()
    out_rows(2)
    total.send_over()
    out_rows(0)
    supply.tick(8)
    spread_mid = Spread(at, full, gs.at[1], gr.at[1])
    for i in range(CHUNKS):
        here = slice(i * step, (i + 1) * step)
        value = tok[here].astype(F32) + (total.take(i) + obias[...])
        mid[here] = value
        unit, _ = unit_rows(value)
        full[here] = (unit * norm_gains[1:2] + norm_shifts[1:2]).astype(BF16)
        spread_mid.post(i)
        if i % 2 == 1:
            supply.tick(9 + i // 2)
    for i in range(CHUNKS):
        spread_mid.forward(i)
        if i == 1:
            supply.tick(11)
    for n in range(12, len(supply.items)):
        supply.tick(n)
    total.finish()
    spread_mid.finish()
    relay.finish(2)
    for k in (5, 6):
        supply.ready(k)
    supply.finish()

    @pl.when(moved)
    def _():
        for i in range(CHUNKS):
            token(i).wait_send()
        for copy in packs():
            copy.wait_send()


def front(ids, tokens, numbers, tables, norm_gains, norm_shifts, obias, w3, wo, wu, wd, cot):
    rows, width = tokens.shape
    n = 4 * rows
    cols = w3.shape[2]
    rank = tables[1].shape[1]
    packed = 4 * cols + 2 * wu.shape[1]
    items = 3 + (wo.shape[0] + wu.shape[0] + wd.shape[0]) // 4 // ITEM + rows // ITEM
    low = lambda *s: jax.ShapeDtypeStruct(s, BF16)
    high = lambda *s: jax.ShapeDtypeStruct(s, F32)
    return pl.pallas_call(
        front_kernel,
        in_specs=[pl.BlockSpec(memory_space=pltpu.SMEM)] + [VMEM_SPEC] * 13 + [ANY_SPEC] * 5,
        out_specs=[VMEM_SPEC] * 12 + [ANY_SPEC] * 5,
        out_shape=[
            low(n, width), low(rows, width), low(rank, packed), high(*numbers.shape), low(4 * rank, width),
            low(n, 3 * cols), high(cols // HEAD_DIM, n), low(n, cols), low(n, rank), low(n, rank),
            low(n, width), high(rows, width), low(n, width), low(*w3.shape), low(*wo.shape), low(*wu.shape), low(*wd.shape),
        ],
        scratch_shapes=[
            VM((rank, packed), BF16),
            VM((n, width), BF16), VM(w3.shape, BF16), VM(wo.shape, BF16), VM((n, rows), F32), VM((cols, n), BF16),
            VM((2 * rows, width), BF16), VM((rows, width), BF16), VM((rows, width), BF16),
        ]
        + sems(CHUNKS) + sems(2) + sems(items) + sems(items, 3) + sems(3, rows // ITEM)
        + sems(3, CHUNKS) + sems(2, 3, CHUNKS) + [pltpu.SemaphoreType.DMA((5,))],
        compiler_params=comm_params(1, 60),
        name="front",
    )(ids, tokens, numbers, *tables, norm_gains, norm_shifts, obias, w3, wo, wu, wd, cot)


class Tables:
    def __init__(self, at, own, shared, own_home, quarter_home, own_all, quarter_all, every, buffers, semaphores):
        self.at, self.own, self.shared = at, own, shared
        self.own_home, self.quarter_home = own_home, quarter_home
        self.own_all, self.quarter_all, self.every = own_all, quarter_all, every
        self.half_in, self.half, self.quarter_in, self.quarter = buffers
        (self.s1, self.r1, self.s2, self.r2, self.s3, self.r3, self.s4, self.r4, self.s5, self.r5, self.s6, self.r6, self.keep) = semaphores
        self.d, self.t = lax.axis_index("dp"), lax.axis_index("tensor")
        self.nd, self.nt = own_all.shape[0], every.shape[0]
        self.core, self.low = self.d % 2, self.t % 2
        self.wide = shared.shape[1] // 2
        self.narrow = self.wide // 2

    def first(self):
        away = pl.ds(pl.multiple_of((1 - self.core) * self.wide, self.wide), self.wide)
        return remote(self.shared.at[:, away], self.half_in, self.s1, self.r1, self.at["core"])

    def second(self):
        away = pl.ds(pl.multiple_of((1 - self.low) * self.narrow, self.narrow), self.narrow)
        return remote(self.half.at[:, away], self.quarter_in, self.s2, self.r2, self.at["near"])

    def third(self):
        return (
            remote(self.own, self.own_home, self.s3.at[0], self.r3.at[0], self.at["cross"]),
            remote(self.quarter, self.quarter_home, self.s3.at[1], self.r3.at[1], self.at["cross"]),
        )

    def fourth(self, k):
        peer = (lax.rem(self.d + k, self.nd), self.t)
        return (
            remote(self.own_home, self.own_all.at[self.d], self.s4.at[0, k], self.r4.at[0, k], peer),
            remote(self.quarter_home, self.quarter_all.at[self.d], self.s4.at[1, k], self.r4.at[1, k], peer),
        )

    def stay(self):
        return (
            pltpu.make_async_copy(self.own_home, self.own_all.at[self.d], self.keep.at[0]),
            pltpu.make_async_copy(self.quarter_home, self.quarter_all.at[self.d], self.keep.at[1]),
        )

    def share_of(self, core):
        return pl.ds(core * (self.nd // 2), self.nd // 2)

    def fifth(self, k):
        peer = (self.d, lax.rem(self.t + k, self.nt))
        slots = self.share_of(self.core)
        return remote(
            self.quarter_all.at[slots], self.every.at[self.t, slots], self.s5.at[k], self.r5.at[k], peer
        )

    def sixth(self, k):
        block = self.every.at[lax.rem(self.t + k, self.nt), self.share_of(self.core)]
        return remote(block, block, self.s6.at[k], self.r6.at[k], self.at["core"])

    def stay_every(self):
        return pltpu.make_async_copy(self.quarter_all, self.every.at[self.t], self.keep.at[2])

    def peers(self, act):
        def body(k, carry):
            for copy in self.fourth(k):
                act(copy)
            return carry

        lax.fori_loop(1, self.nd, body, 0)

    def hop1(self):
        self.first().start()

    def hop2(self):
        self.first().wait_recv()
        mine = pl.ds(pl.multiple_of(self.core * self.wide, self.wide), self.wide)
        self.half[...] = (self.shared[:, mine].astype(F32) + self.half_in[...].astype(F32)).astype(BF16)
        self.second().start()

    def hop3(self):
        self.second().wait_recv()
        mine = pl.ds(pl.multiple_of(self.low * self.narrow, self.narrow), self.narrow)
        self.quarter[...] = (self.half[:, mine].astype(F32) + self.quarter_in[...].astype(F32)).astype(BF16)

        @pl.when(self.at["moved"])
        def _():
            for copy in self.third():
                copy.start()

        @pl.when(jnp.logical_not(self.at["moved"]))
        def _():
            self.own_home[...] = self.own[...]
            self.quarter_home[...] = self.quarter[...]

    def hop4(self):
        @pl.when(self.at["moved"])
        def _():
            for copy in self.third():
                copy.wait_recv()

        for copy in self.stay():
            copy.start()
        self.peers(lambda copy: copy.start())

    def hop5(self):
        self.peers(lambda copy: copy.wait_recv())
        for copy in self.stay():
            copy.wait()
        self.stay_every().start()
        for k in range(1, self.nt):
            self.fifth(k).start()

    def hop6(self):
        for k in range(1, self.nt):
            self.fifth(self.nt - k).wait_recv()
            self.sixth(k).start()

    def finish(self):
        self.first().wait_send()
        self.second().wait_send()

        @pl.when(self.at["moved"])
        def _():
            for copy in self.third():
                copy.wait_send()

        self.peers(lambda copy: copy.wait_send())
        self.stay_every().wait()
        for k in range(1, self.nt):
            self.fifth(k).wait_send()
            self.sixth(k).wait()


def tables_scratch(nd, rank, own, count, width):
    rows = count * rank
    return (
        [
            VM((rank, own), BF16), VM((rows, width), BF16), VM((rank, own), BF16), VM((rows, width // 4), BF16),
            VM((nd, rows, width // 4), BF16),
            VM((rows, width // 2), BF16), VM((rows, width // 2), BF16), VM((rows, width // 4), BF16),
            VM((rows, width // 4), BF16),
        ],
        [pltpu.SemaphoreType.DMA] * 4 + sems(2) + sems(2, nd) + sems(4) + sems(4) + [pltpu.SemaphoreType.DMA((3,))],
    )


def back_kernel(
    gmid, mlp_part, x, w3, wqkv, wo, wo_role, cot, mid, tok, gains, dbias, proj, ctx, lse, rank_qkv, rank_out,
    small, chosen, nums, tuo, tdi, tui, tdo, ids,
    out, in_grad, own_early, every_early, own_late, every_late, all_ids,
    work, kept, gm, grad, gctx, gproj, dist, kt, gk, gv, wv, wov, side, far, mix, side2, far2, mix2, done, done2,
    *rest,
):
    early_buffers, late_buffers = rest[:9], rest[9:18]
    early_sems, late_sems = rest[18:31], rest[31:44]
    rs, rr, ms, mr, ls, lr, gs, gr, os, orr, bs, br, ns, nr, load = rest[44:]
    at = places()
    moved = at["moved"]
    still = jnp.logical_not(moved)
    d, t = lax.axis_index("dp"), lax.axis_index("tensor")
    nd, nt = own_early.shape[0], every_early.shape[0]
    barrier = pltpu.get_barrier_semaphore()

    def hail(k, carry):
        pl.semaphore_signal(barrier, inc=1, device_id=(lax.rem(d + k, nd), t), device_id_type=MESH)
        return carry

    lax.fori_loop(1, nd, hail, 0)
    for k in range(1, nt):
        pl.semaphore_signal(barrier, inc=1, device_id=(d, lax.rem(t + k, nt)), device_id_type=MESH)

    @pl.when(moved)
    def _():
        pl.semaphore_signal(barrier, inc=1, device_id=at["cross"], device_id_type=MESH)

    pl.semaphore_wait(barrier, nd - 1 + nt - 1 + moved.astype(jnp.int32))

    rows = tok.shape[0]
    step = rows // CHUNKS
    cols = ctx.shape[1]
    rank = small.shape[0]
    heads = cols // HEAD_DIM
    scale = 1.0 / math.sqrt(HEAD_DIM)
    get_work = pltpu.make_async_copy(gmid, work, load.at[0])
    get_work.start()
    get_kept = [
        pltpu.make_async_copy(mlp_part.at[pl.ds(2 * j * rows, rows)], kept.at[pl.ds(j * rows, rows)], load.at[1 + j])
        for j in range(2)
    ]
    for copy in get_kept:
        copy.start()
    fetch(wo, wo_role, wov, load.at[3])
    all_ids[d] = ids[...]

    def number(k):
        return remote(ids, all_ids.at[d], ns.at[k], nr.at[k], (lax.rem(d + k, nd), t))

    def send_number(k, carry):
        number(k).start()
        return carry

    def await_number(k, carry):
        number(k).wait()
        return carry

    get_work.wait()
    total = Gathered(at, work, side, far, mix, rs, rr)
    spread = Spread(at, gm, gs, gr)
    total.begin()
    own, shared, own_home, quarter_home, quarter_all = early_buffers[:5]
    wide = tuo.shape[1]
    own[:, :wide] = tuo[...].astype(BF16)
    own[:, wide:] = tdi[...].astype(BF16)
    shared[0:rank] = tui[...].astype(BF16)
    shared[rank : 2 * rank] = tdo[...].astype(BF16)
    early = Tables(
        at, own, shared, own_home, quarter_home, own_early, quarter_all, every_early, early_buffers[5:], early_sems
    )
    early.hop1()
    lax.fori_loop(1, nd, send_number, 0)
    for i in range(CHUNKS):
        here = slice(i * step, (i + 1) * step)
        unit, inverse = unit_rows(mid[here])
        value = cot[here].astype(F32) + unit_back(total.take(i), unit, inverse, gains[1:2])
        grad[here] = value
        gm[here] = value.astype(BF16)
        spread.post(i)
    early.hop2()
    for i in range(CHUNKS):
        spread.forward(i)
    early.hop3()
    spread.finish()
    total.finish()

    for copy in get_kept:
        copy.wait()
    mlp = Gathered(at, mlp_part, side, far, mix, ms, mr, kept)
    mlp.send_away()
    mlp.send_home()
    pltpu.make_async_copy(wo, wov, load.at[3]).wait()
    bq, ao = small[:, : 3 * cols], small[:, 3 * cols : 4 * cols]
    aq, bo = chosen[0:rank], chosen[rank : 2 * rank]

    def context_rows(i, sums):
        here = pl.ds(i * rows, rows)
        g = gm[here]
        r = dot_t(g, bo).astype(BF16)
        gctx[here] = (dot_t(g, wov[...]) + dot(r, ao)).astype(BF16)
        return sums[0] + t_dot(rank_out[here], g), sums[1] + t_dot(r, ctx[here])

    sums = (jnp.zeros((rank, gm.shape[1]), F32), jnp.zeros((rank, cols), F32))
    sums = context_rows(0, sums)
    mlp.send_over()
    early.hop4()
    for i in range(1, 4):
        sums = context_rows(i, sums)
    early.hop5()
    context_sums = sums
    get_x = pltpu.make_async_copy(x, gm, load.at[4])
    get_x.start()
    for j in range(3):
        fetch(w3.at[j], wqkv.at[j], wv.at[j], load.at[5 + j])

    me = 2 * (d % 2) + t % 2
    base = nums.shape[1] - 128
    slopes = head_slopes(me, heads)
    kt[...] = proj[:, cols : 2 * cols].T
    gk[...] = jnp.zeros_like(gk)
    gv[...] = jnp.zeros_like(gv)

    def attend_step(i, carry):
        here = pl.ds(pl.multiple_of(i * rows, rows), rows)
        distances(me, nums[0:1, base : base + 1], nums[0:1, base + 1 : base + 2], rows, i, dist)
        for h in range(heads):
            span = slice(h * HEAD_DIM, (h + 1) * HEAD_DIM)
            q, g = proj[here, span], gctx[here, span]
            keys = proj[:, cols + h * HEAD_DIM : cols + (h + 1) * HEAD_DIM]
            values = proj[:, 2 * cols + h * HEAD_DIM : 2 * cols + (h + 1) * HEAD_DIM]
            s = dot_t(keys, q) * (scale * LOG2E) - dist[...] * slopes[h]
            p = jnp.exp2(s - lse[h : h + 1, here])
            gv[:, span] += dot(p.astype(BF16), g)
            gp = dot_t(values, g)
            inner = jnp.sum(p * gp, axis=0, keepdims=True)
            gsc = (p * (gp - inner)).astype(BF16)
            gk[:, span] += dot(gsc, q)
            gproj[here, span] = (dot(kt[span, :], gsc).T * scale).astype(BF16)
        return carry

    lax.fori_loop(0, 2, attend_step, 0)
    early.hop6()
    lax.fori_loop(2, 4, attend_step, 0)
    gproj[:, cols : 2 * cols] = (gk[...] * scale).astype(BF16)
    gproj[:, 2 * cols :] = gv[...].astype(BF16)

    def out_back(i):
        here = pl.ds(i * step, step)
        return remote(done.at[here], out.at[here], os.at[i], orr.at[i], at["cross"])

    def grad_back(i):
        here = pl.ds(i * step, step)
        return remote(done2.at[here], in_grad.at[here], bs.at[i], br.at[i], at["cross"])

    for i in range(CHUNKS):
        here = slice(i * step, (i + 1) * step)
        value = (mid[here] + (mlp.take(i) + dbias[...])).astype(BF16)

        @pl.when(moved)
        def _():
            done[here] = value
            out_back(i).start()

        @pl.when(still)
        def _():
            out[here] = value

    get_x.wait()
    for j in range(3):
        pltpu.make_async_copy(w3.at[j], wv.at[j], load.at[5 + j]).wait()
    own, shared, own_home, quarter_home, quarter_all = late_buffers[:5]

    def input_rows(i, sums):
        here = pl.ds(i * rows, rows)
        g = gproj[here]
        r = dot_t(g, bq).astype(BF16)
        acc = dot(r, aq)
        for j in range(3):
            acc = acc + dot_t(g[:, j * cols : (j + 1) * cols], wv[j])
        work[here] = acc.astype(BF16)
        return sums[0] + t_dot(rank_qkv[here], g), sums[1] + t_dot(r, gm[here])

    last = Gathered(at, work, side2, far2, mix2, ls, lr)
    sums = (jnp.zeros((rank, 3 * cols), F32), jnp.zeros((rank, gm.shape[1]), F32))
    sums = input_rows(3, sums)
    last.send_away()
    sums = input_rows(1, sums)
    last.send_home()
    sums = input_rows(2, sums)
    last.send_over()
    sums = input_rows(0, sums)
    own[:, : 3 * cols] = sums[0].astype(BF16)
    own[:, 3 * cols :] = context_sums[1].astype(BF16)
    shared[0:rank] = sums[1].astype(BF16)
    shared[rank : 2 * rank] = context_sums[0].astype(BF16)
    late = Tables(at, own, shared, own_home, quarter_home, own_late, quarter_all, every_late, late_buffers[5:], late_sems)
    late.hop1()
    hops = (late.hop2, late.hop3, late.hop4, late.hop5)
    for i in range(CHUNKS):
        here = slice(i * step, (i + 1) * step)
        unit, inverse = unit_rows(tok[here].astype(F32))
        value = (grad[here] + unit_back(last.take(i), unit, inverse, gains[0:1])).astype(BF16)

        @pl.when(moved)
        def _():
            done2[here] = value
            grad_back(i).start()

        @pl.when(still)
        def _():
            in_grad[here] = value

        hops[i]()
    late.hop6()
    lax.fori_loop(1, nd, await_number, 0)
    mlp.finish()
    last.finish()
    early.finish()
    late.finish()

    @pl.when(moved)
    def _():
        for i in range(CHUNKS):
            out_back(i).wait()
            grad_back(i).wait()


def back(nd, nt, gmid, mlp_part, x, w3, wqkv, wo, wo_role, cot, mid, tok, gains, dbias, proj, ctx, lse, rank_qkv,
         rank_out, small, chosen, nums, tuo, tdi, tui, tdo, ids):
    rows, width = tok.shape
    n = 4 * rows
    cols = ctx.shape[1]
    rank = small.shape[0]
    early_own = 2 * tuo.shape[1]
    low = lambda *s: jax.ShapeDtypeStruct(s, BF16)
    early = tables_scratch(nd, rank, early_own, 2, width)
    late = tables_scratch(nd, rank, 4 * cols, 2, width)
    return pl.pallas_call(
        back_kernel,
        in_specs=[ANY_SPEC] * 7 + [VMEM_SPEC] * 18,
        out_specs=[VMEM_SPEC] * 2 + [ANY_SPEC] * 4 + [VMEM_SPEC],
        out_shape=[
            low(rows, width), low(rows, width),
            low(nd, rank, early_own), low(nt, nd, 2 * rank, width // 4),
            low(nd, rank, 4 * cols), low(nt, nd, 2 * rank, width // 4),
            jax.ShapeDtypeStruct((nd,) + ids.shape, jnp.int32),
        ],
        scratch_shapes=[
            VM((n, width), BF16), VM((2 * rows, width), BF16), VM((n, width), BF16), VM((rows, width), F32),
            VM((n, cols), BF16), VM((n, 3 * cols), BF16), VM((n, rows), F32), VM((cols, n), BF16),
            VM((n, cols), F32), VM((n, cols), F32), VM(w3.shape, BF16), VM(wo.shape, BF16),
            VM((2 * rows, width), BF16), VM((rows, width), BF16), VM((rows, width), BF16),
            VM((2 * rows, width), BF16), VM((rows, width), BF16), VM((rows, width), BF16),
            VM((rows, width), BF16), VM((rows, width), BF16),
        ]
        + early[0] + late[0] + early[1] + late[1]
        + sems(3, CHUNKS) * 4 + sems(CHUNKS) * 2 + sems(nd) + [pltpu.SemaphoreType.DMA((8,))],
        compiler_params=comm_params(2, 62),
        name="back",
    )(gmid, mlp_part, x, w3, wqkv, wo, wo_role, cot, mid, tok, gains, dbias, proj, ctx, lse, rank_qkv, rank_out,
      small, chosen, nums, tuo, tdi, tui, tdo, ids)


def combine_kernel(ids, own_early, every_early, own_late, every_late, gqi, gqo, goi, goo, gui, guo, gdi, gdo):
    nd = own_early.shape[0]
    cols = goi.shape[2]
    wide = guo.shape[2]
    rank = goi.shape[1]
    quarter = every_late.shape[3]
    for ref in (gqi, gqo, goi, goo, gui, guo, gdi, gdo):
        ref[...] = jnp.zeros_like(ref)

    def add(s, carry):
        e = [ids[s, 0, k] for k in range(4)]
        for j in range(3):
            gqo[e[0], j] += own_late[s, :, j * cols : (j + 1) * cols].astype(F32)
        goi[e[1]] += own_late[s, :, 3 * cols :].astype(F32)
        guo[e[2]] += own_early[s, :, :wide].astype(F32)
        gdi[e[3]] += own_early[s, :, wide:].astype(F32)
        for z in range(every_late.shape[0]):
            at = slice(z * quarter, (z + 1) * quarter)
            gqi[e[0], :, at] += every_late[z, s, 0:rank].astype(F32)
            goo[e[1], :, at] += every_late[z, s, rank:].astype(F32)
            gui[e[2], :, at] += every_early[z, s, 0:rank].astype(F32)
            gdo[e[3], :, at] += every_early[z, s, rank:].astype(F32)
        return carry

    lax.fori_loop(0, nd, add, 0)


def combine(ids, own_early, every_early, own_late, every_late, tables, cols, wide):
    rank = own_early.shape[1]
    width = every_late.shape[0] * every_late.shape[3]
    high = lambda *s: jax.ShapeDtypeStruct(s, F32)
    full = high(tables, rank, width)
    return pl.pallas_call(
        combine_kernel,
        in_specs=[pl.BlockSpec(memory_space=pltpu.SMEM)] + [VMEM_SPEC] * 4,
        out_specs=[VMEM_SPEC] * 8,
        out_shape=[
            full, high(tables, 3, rank, cols), high(tables, rank, cols), full, full, high(tables, rank, wide),
            high(tables, rank, wide), full,
        ],
        compiler_params=params(48),
        name="combine",
    )(ids, own_early, every_early, own_late, every_late)


def body(
    tokens, cotangent, norm_gains, norm_shifts, query_key_value_weight, b_qv, output_weight,
    output_bias_vector, up_weight, b_up, down_weight, down_bias_vector, adapter_query_key_value_input,
    qkv_out, adapter_output_input, adapter_output_output, adapter_up_input, up_out, down_in,
    adapter_down_output, offsets, adapter_ids,
):
    nd, nt = lax.axis_size("dp"), lax.axis_size("tensor")
    rows, width = tokens.shape
    local = output_weight.shape[0]
    hidden_width = up_weight.shape[1]
    tables = adapter_up_input.shape[0]

    w3 = jnp.transpose(query_key_value_weight, (1, 0, 2))
    b3 = jnp.transpose(qkv_out, (0, 2, 1, 3))
    extra = jnp.pad(jnp.concatenate([offsets, adapter_ids], 1).astype(F32), ((0, 0), (0, 122)))
    numbers = jnp.concatenate([b_qv.reshape(1, 2 * local), b_up.reshape(1, hidden_width), extra], 1)
    tables_in = (
        b3, adapter_output_input, up_out, down_in, adapter_query_key_value_input, adapter_output_output,
        adapter_up_input, adapter_down_output,
    )
    (
        x, tok, small, nums, chosen, proj, lse, ctx, rank_qkv, rank_out, nm, middle, cot, wqkv, wo, wu, wd,
    ) = front(
        adapter_ids[0], tokens, numbers, tables_in, norm_gains, norm_shifts, output_bias_vector.reshape(1, width),
        w3, output_weight, up_weight, down_weight, cotangent,
    )
    part, gmid, t_up_out, t_down_in, t_up_in, t_down_out = mlp(
        nm, cot, up_weight, wu, down_weight, wd, chosen, small, nums, hidden_width // 4
    )
    result, in_grad, own_early, every_early, own_late, every_late, everyone = back(
        nd, nt, gmid, part, x, w3, wqkv, output_weight, wo, cot[:rows], middle, tok, norm_gains,
        down_bias_vector.reshape(1, width), proj, ctx, lse, rank_qkv, rank_out, small, chosen, nums,
        t_up_out, t_down_in, t_up_in, t_down_out, jnp.pad(adapter_ids, ((0, 0), (0, 124))),
    )
    gqi, gqo, goi, goo, gui, guo, gdi, gdo = combine(
        everyone, own_early, every_early, own_late, every_late, tables, local, hidden_width
    )
    return (result, in_grad, gqi, jnp.transpose(gqo, (0, 2, 1, 3)), goi, goo, gui, guo, gdi, gdo)


def solution(mesh):
    placed = (
        P(("dp", "tensor"), None), P(("dp", "tensor"), None), P(), P(), P(None, None, "tensor"), P(None, "tensor"),
        P("tensor", None), P(), P(None, "tensor"), P("tensor"), P("tensor", None), P(), P(),
        P(None, None, None, "tensor"), P(None, None, "tensor"), P(), P(), P(None, None, "tensor"),
        P(None, None, "tensor"), P(), P("dp", None), P("dp", None),
    )
    return jax.shard_map(
        body, mesh=mesh, in_specs=placed,
        out_specs=(
            P(("dp", "tensor"), None), P(("dp", "tensor"), None), P(), P(None, None, None, "tensor"),
            P(None, None, "tensor"), P(), P(), P(None, None, "tensor"), P(None, None, "tensor"), P(),
        ),
        check_vma=False,
    )
```

```python
import functools
import math

import jax
import jax.numpy as jnp
from jax import lax
from jax.experimental import pallas as pl
from jax.experimental.pallas import tpu as pltpu
from jax.sharding import PartitionSpec as P

HEADS = 16
HEAD_DIM = 128
PIECE = 256
ITEM = 128
AHEAD = 2
EPS = 1e-05
GELU_C = 0.7978845608028654
GELU_K = 0.044715
LOG2E = 1.4426950408889634
FAR = 1e32
F32 = jnp.float32
BF16 = jnp.bfloat16
AXES = ("dp", "tensor")
VM = pltpu.VMEM
HERE = pl.BlockSpec(memory_space=pl.ANY)


def dot(a, b):
    return lax.dot_general(a, b, (((1,), (0,)), ((), ())), preferred_element_type=F32)


def dot_t(a, b):
    return lax.dot_general(a, b, (((1,), (1,)), ((), ())), preferred_element_type=F32)


def t_dot(a, b):
    return lax.dot_general(a, b, (((0,), (0,)), ((), ())), preferred_element_type=F32)


def whole(shape):
    zeros = (0,) * len(shape)
    return pl.BlockSpec(shape, lambda *_: zeros)


def params(mib=56):
    return pltpu.CompilerParams(vmem_limit_bytes=mib << 20)


def cost(flops, read):
    return pl.CostEstimate(flops=int(flops), bytes_accessed=int(read), transcendentals=0)


def displaced():
    return (lax.axis_index("dp") % 2 + lax.axis_index("tensor") // 2) % 2 == 1


def fetch(native, brought, into, sem):
    moved = displaced()

    @pl.when(moved)
    def _():
        pltpu.make_async_copy(brought, into, sem).start()

    @pl.when(jnp.logical_not(moved))
    def _():
        pltpu.make_async_copy(native, into, sem).start()

    return pltpu.make_async_copy(native, into, sem)


def distances(me, s0, s1, rows, step, dist):
    length = dist.shape[0]

    def piece(pos, none):
        one = jnp.where((pos >= s0) & (pos < s0 + PIECE), 1.0, none)
        return jnp.where((pos >= s1) & (pos < s1 + PIECE), 2.0, one)

    def rel(j):
        return ((j & 1) << 1) | (j >> 1)

    i = lax.broadcasted_iota(jnp.int32, (length, 128), 0)
    kpos = ((me ^ rel(i // rows)) * rows + i % rows).astype(F32)[:, :1]
    qpos = ((me ^ rel(step)) * rows + lax.broadcasted_iota(jnp.int32, (1, rows), 1)).astype(F32)
    seen = (kpos <= qpos) | (piece(kpos, -1.0) == piece(qpos, -2.0))
    dist[...] = jnp.where(seen, jnp.abs(kpos - qpos), FAR)


def head_slopes(me, heads):
    first = jnp.full((1, 1), me * heads, jnp.int32).astype(F32)
    return [jnp.exp2((first + float(h + 1)) * (-8.0 / HEADS)) * LOG2E for h in range(heads)]


def gelu_parts(values):
    square = values * values
    tangent = jnp.tanh(GELU_C * (values + GELU_K * square * values))
    half = 0.5 * (1.0 + tangent)
    slope = half + (0.5 * GELU_C) * values * (1.0 - tangent * tangent) * (1.0 + 3.0 * GELU_K * square)
    return values * half, slope


MESH = pl.DeviceIdType.MESH
CHUNKS = 4


def places():
    d, t = lax.axis_index("dp"), lax.axis_index("tensor")
    core, zh = d % 2, t // 2
    core_d = d + 1 - 2 * core
    near_t = t + 1 - 2 * (t % 2)
    left = d + 2 - 4 * ((d // 2) % 2)
    up = 4 - 8 * ((d // 4) % 2)
    return dict(
        moved=(core + zh) % 2 == 1,
        line=(d // 2) % 4,
        core=(core_d, t),
        near=(d, near_t),
        cross=(core_d, t + 2 - 4 * zh),
        left=(left, t),
        up=(d + up, t),
        both=(left + up, t),
    )


def greet(always, sometimes=(), when=None):
    barrier = pltpu.get_barrier_semaphore()
    for peer in always:
        pl.semaphore_signal(barrier, inc=1, device_id=peer, device_id_type=MESH)
    count = len(always)
    if sometimes:

        @pl.when(when)
        def _():
            for peer in sometimes:
                pl.semaphore_signal(barrier, inc=1, device_id=peer, device_id_type=MESH)

        count = count + len(sometimes) * when.astype(jnp.int32)
    pl.semaphore_wait(barrier, count)


def remote(src, dst, send, recv, peer):
    return pltpu.make_async_remote_copy(
        src_ref=src, dst_ref=dst, send_sem=send, recv_sem=recv, device_id=peer, device_id_type=MESH
    )


def unit_rows(v):
    centre = v - jnp.mean(v, axis=-1, keepdims=True)
    inverse = lax.rsqrt(jnp.mean(centre * centre, axis=-1, keepdims=True) + EPS)
    return centre * inverse, inverse


def unit_back(grad, scaled, inverse, gain):
    inner = grad * gain
    first = jnp.mean(inner, axis=-1, keepdims=True)
    second = jnp.mean(inner * scaled, axis=-1, keepdims=True)
    return inverse * (inner - first - scaled * second)


class Spread:
    def __init__(self, at, full, send, recv):
        self.at, self.full, self.send, self.recv = at, full, send, recv
        self.rows = full.shape[0] // 4
        self.step = self.rows // CHUNKS
        self.waited = False

    def block(self, k, i):
        return self.full.at[pl.ds(k * self.rows + i * self.step, self.step)]

    def side(self, i):
        return remote(self.block(0, i), self.block(1, i), self.send.at[0, i], self.recv.at[0, i], self.at["core"])

    def far(self, i):
        return remote(self.block(0, i), self.block(2, i), self.send.at[1, i], self.recv.at[1, i], self.at["near"])

    def onward(self, i):
        return remote(self.block(2, i), self.block(3, i), self.send.at[2, i], self.recv.at[2, i], self.at["core"])

    def post(self, i):
        self.far(i).start()
        self.side(i).start()

    def forward(self, i):
        self.far(i).wait_recv()
        self.onward(i).start()

    def beside(self):
        for i in range(CHUNKS):
            self.side(i).wait_recv()
        self.waited = True

    def finish(self):
        for i in range(CHUNKS):
            if not self.waited:
                self.side(i).wait_recv()
            self.side(i).wait_send()
            self.far(i).wait_send()
            self.onward(i).wait()


class Gathered:
    def __init__(self, at, part, side, far, mix, send, recv, kept=None):
        self.at, self.part, self.side, self.far, self.mix = at, part, side, far, mix
        self.kept, self.second = (part, 2) if kept is None else (kept, 1)
        self.send, self.recv = send, recv
        self.rows = part.shape[0] // 4
        self.step = self.rows // CHUNKS

    def away(self, i):
        src = self.part.at[pl.ds(3 * self.rows + i * self.step, self.step)]
        dst = self.side.at[pl.ds(self.rows + i * self.step, self.step)]
        return remote(src, dst, self.send.at[0, i], self.recv.at[0, i], self.at["core"])

    def home(self, i):
        src = self.part.at[pl.ds(self.rows + i * self.step, self.step)]
        dst = self.side.at[pl.ds(i * self.step, self.step)]
        return remote(src, dst, self.send.at[1, i], self.recv.at[1, i], self.at["core"])

    def over(self, i):
        here = pl.ds(i * self.step, self.step)
        return remote(self.mix.at[here], self.far.at[here], self.send.at[2, i], self.recv.at[2, i], self.at["near"])

    def send_away(self):
        for i in range(CHUNKS):
            self.away(i).start()

    def send_home(self):
        for i in range(CHUNKS):
            self.home(i).start()

    def send_over(self):
        for i in range(CHUNKS):
            self.away(i).wait_recv()
            here = pl.ds(i * self.step, self.step)
            ours = self.kept[pl.ds(self.second * self.rows + i * self.step, self.step)].astype(F32)
            theirs = self.side[pl.ds(self.rows + i * self.step, self.step)].astype(F32)
            self.mix[here] = (ours + theirs).astype(BF16)
            self.over(i).start()

    def begin(self):
        self.send_away()
        self.send_home()
        self.send_over()

    def take(self, i):
        self.home(i).wait_recv()
        self.over(i).wait_recv()
        here = pl.ds(i * self.step, self.step)
        return self.kept[here].astype(F32) + self.side[here].astype(F32) + self.far[here].astype(F32)

    def finish(self):
        for i in range(CHUNKS):
            self.away(i).wait_send()
            self.home(i).wait_send()
            self.over(i).wait_send()


def sems(*shape):
    return [pltpu.SemaphoreType.DMA(shape), pltpu.SemaphoreType.DMA(shape)]


def comm_params(number, mib=56):
    return pltpu.CompilerParams(collective_id=number, has_side_effects=True, vmem_limit_bytes=mib << 20)


VMEM_SPEC = pl.BlockSpec(memory_space=pltpu.VMEM)
ANY_SPEC = pl.BlockSpec(memory_space=pl.ANY)


class Supply:
    def __init__(self, at, plan, cross_send, cross_recv, share_send, share_recv):
        self.at, self.plan = at, plan
        self.xs, self.xr, self.ss, self.sr = cross_send, cross_recv, share_send, share_recv
        self.moved = at["moved"]
        self.peers = (at["left"], at["up"], at["both"])
        self.items = []
        for k, (native, role, shared, span) in enumerate(plan):
            size = native.shape[0] // 4 if shared else native.shape[0]
            for i in range(size // span):
                self.items.append((k, size, i))

    def rows(self, n):
        k, size, i = self.items[n]
        span = self.plan[k][3]
        if self.plan[k][2]:
            return pl.ds(pl.multiple_of(self.at["line"] * size + i * span, span), span)
        return pl.ds(i * span, span)

    def cross(self, n):
        native, role = self.plan[self.items[n][0]][:2]
        return remote(native.at[self.rows(n)], role.at[self.rows(n)], self.xs.at[n], self.xr.at[n], self.at["cross"])

    def share(self, n, k):
        role = self.plan[self.items[n][0]][1]
        block = role.at[self.rows(n)]
        return remote(block, block, self.ss.at[n, k], self.sr.at[n, k], self.peers[k])

    def begin(self, ahead):
        for n in range(ahead):
            self.cross(n).start()
        self.ahead = ahead

    def tick(self, n):
        @pl.when(self.moved)
        def _():
            self.cross(n).wait_recv()
            if n + self.ahead < len(self.items):
                self.cross(n + self.ahead).start()
            if self.plan[self.items[n][0]][2]:
                for k in range(3):
                    self.share(n, k).start()

    def ready(self, k):
        @pl.when(self.moved)
        def _():
            for n, item in enumerate(self.items):
                if item[0] == k:
                    for j in range(3):
                        self.share(n, j).wait_recv()

    def ready_item(self, n):
        @pl.when(self.moved)
        def _():
            for j in range(3):
                self.share(n, j).wait_recv()

    def finish(self):
        @pl.when(self.moved)
        def _():
            for n, item in enumerate(self.items):
                self.cross(n).wait_send()
                if self.plan[item[0]][2]:
                    for j in range(3):
                        self.share(n, j).wait_send()


class Relay:
    def __init__(self, at, full, send, recv):
        self.at, self.full, self.send, self.recv = at, full, send, recv
        self.rows = full.shape[0] // 4

    def block(self, k, i):
        return self.full.at[pl.ds(k * self.rows + i * ITEM, ITEM)]

    def side(self, i):
        return remote(self.block(0, i), self.block(1, i), self.send.at[0, i], self.recv.at[0, i], self.at["core"])

    def far(self, i):
        return remote(self.block(0, i), self.block(2, i), self.send.at[1, i], self.recv.at[1, i], self.at["near"])

    def last(self, i):
        return remote(self.block(2, i), self.block(3, i), self.send.at[2, i], self.recv.at[2, i], self.at["core"])

    def post(self, i):
        self.far(i).start()
        self.side(i).start()

    def forward(self, i):
        self.far(i).wait_recv()
        self.last(i).start()

    def finish(self, count):
        for i in range(count):
            self.side(i).wait()
            self.far(i).wait_send()
            self.last(i).wait()


def pick_row(table, key):
    total = jnp.zeros(table.shape[1:], F32)
    for e in range(table.shape[0]):
        total = total + jnp.where(key == float(e), table[e].astype(F32), 0.0)
    return total.astype(BF16)


def front_kernel(
    ids, tokens, numbers, t_bq, t_ao, t_bu, t_ad, t_aq, t_bo, t_au, t_bd, norm_gains, norm_shifts, obias,
    w3, wo, wu, cot,
    x, tok, small, nums, chosen, proj, lse, ctx, rank_qkv, rank_out, full, mid, cot_full, wqkv, wo_role, wu_role,
    small_own, part, wv, wov, dist, vt, side, far, mix,
    ts, tr, ps, pr, xs, xr, ss, sr, cs, cr, rs, rr, gs, gr, load,
):
    at = places()
    moved = at["moved"]
    still = jnp.logical_not(moved)
    rows = tok.shape[0]
    step = rows // CHUNKS
    cols = wov.shape[0]
    rank = small.shape[0]
    greet((at["core"], at["near"]), (at["cross"], at["left"], at["up"], at["both"]), moved)
    qkv_span = w3.shape[1] // 4
    supply = Supply(
        at,
        [(w3.at[j], wqkv.at[j], True, qkv_span) for j in range(3)]
        + [(wo, wo_role, True, ITEM), (cot, cot_full, False, ITEM), (wu, wu_role, True, ITEM)],
        xs, xr, ss, sr,
    )
    relay = Relay(at, cot_full, cs, cr)

    def token(i):
        here = pl.ds(i * step, step)
        return remote(tokens.at[here], tok.at[here], ts.at[i], tr.at[i], at["cross"])

    def packs():
        return (
            remote(small_own, small, ps.at[0], pr.at[0], at["cross"]),
            remote(numbers, nums, ps.at[1], pr.at[1], at["cross"]),
        )

    @pl.when(moved)
    def _():
        for i in range(CHUNKS):
            token(i).start()
        supply.begin(AHEAD)

    for j in range(3):
        small_own[:, j * cols : (j + 1) * cols] = t_bq[ids[0], j]
    at_col = 3 * cols
    small_own[:, at_col : at_col + cols] = t_ao[ids[1]]
    at_col += cols
    wide = t_bu.shape[2]
    small_own[:, at_col : at_col + wide] = t_bu[ids[2]]
    at_col += wide
    small_own[:, at_col : at_col + wide] = t_ad[ids[3]]
    get_c = pltpu.make_async_copy(cot, cot_full.at[pl.ds(0, rows)], load.at[4])

    @pl.when(moved)
    def _():
        for copy in packs():
            copy.start()

    @pl.when(still)
    def _():
        get_c.start()
        tok[...] = tokens[...]
        small[...] = small_own[...]
        nums[...] = numbers[...]

    spread = Spread(at, x, gs.at[0], gr.at[0])
    for i in range(CHUNKS):
        here = slice(i * step, (i + 1) * step)

        @pl.when(moved)
        def _():
            token(i).wait_recv()

        unit, _ = unit_rows(tok[here].astype(F32))
        x[here] = (unit * norm_gains[0:1] + norm_shifts[0:1]).astype(BF16)
        spread.post(i)
    supply.tick(0)

    @pl.when(moved)
    def _():
        for copy in packs():
            copy.wait_recv()

    base = 2 * cols + wide
    key = lambda k: nums[0:1, base + k : base + k + 1]
    for k, table in enumerate((t_aq, t_bo, t_au, t_bd)):
        chosen[k * rank : (k + 1) * rank] = pick_row(table, key(2 + k))
    for i in range(CHUNKS):
        spread.forward(i)
    supply.tick(1)
    spread.finish()
    supply.tick(2)
    aq, bo = chosen[0:rank], chosen[rank : 2 * rank]
    rank_qkv[...] = dot_t(x[...], aq).astype(BF16)
    for j in range(3):
        supply.ready(j)
        fetch(w3.at[j], wqkv.at[j], wv.at[j], load.at[j]).wait()
        span = slice(j * cols, (j + 1) * cols)

        def strip(i, carry):
            here = pl.ds(pl.multiple_of(2 * i * rows, 2 * rows), 2 * rows)
            value = dot(x[here], wv[j]) + dot(rank_qkv[here], small[:, span])
            if j != 1:
                value = value + nums[0:1, (j // 2) * cols : (j // 2 + 1) * cols]
            proj[here, span] = value.astype(BF16)
            return carry

        lax.fori_loop(0, 2, strip, 0)
    supply.tick(3)
    me = 2 * (lax.axis_index("dp") % 2) + lax.axis_index("tensor") % 2
    vt[...] = proj[:, 2 * cols :].T
    scale = LOG2E / math.sqrt(HEAD_DIM)
    slopes = head_slopes(me, cols // HEAD_DIM)

    def attend_step(i, carry):
        here = pl.ds(pl.multiple_of(i * rows, rows), rows)
        distances(me, key(0), key(1), rows, i, dist)
        for h in range(cols // HEAD_DIM):
            span = slice(h * HEAD_DIM, (h + 1) * HEAD_DIM)
            keys = proj[:, cols + h * HEAD_DIM : cols + (h + 1) * HEAD_DIM]
            s = dot_t(keys, proj[here, span]) * scale - dist[...] * slopes[h]
            peak = jnp.max(s, axis=0, keepdims=True)
            e = jnp.exp2(s - peak)
            total = jnp.sum(e, axis=0, keepdims=True)
            c = dot(vt[span, :], e.astype(BF16)) * (1.0 / total)
            ctx[here, span] = c.T.astype(BF16)
            lse[h : h + 1, here] = peak + jnp.log2(total)
        return carry

    def attend(first, count):
        lax.fori_loop(first, first + count, attend_step, 0)

    attend(0, 1)
    supply.tick(4)

    @pl.when(still)
    def _():
        get_c.wait()

    relay.post(0)
    attend(1, 1)
    supply.tick(5)
    relay.post(1)
    attend(2, 1)
    supply.tick(6)
    relay.forward(0)
    attend(3, 1)
    supply.tick(7)
    relay.forward(1)
    supply.ready(3)
    fetch(wo, wo_role, wov, load.at[3]).wait()
    ao = small[:, 3 * cols : 4 * cols]

    def out_rows(i):
        here = pl.ds(i * rows, rows)
        r = dot_t(ctx[here], ao).astype(BF16)
        rank_out[here] = r
        part[here] = (dot(ctx[here], wov[...]) + dot(r, bo)).astype(BF16)

    total = Gathered(at, part, side, far, mix, rs, rr)
    out_rows(3)
    total.send_away()
    out_rows(1)
    total.send_home()
    out_rows(2)
    total.send_over()
    out_rows(0)
    supply.tick(8)
    spread_mid = Spread(at, full, gs.at[1], gr.at[1])
    for i in range(CHUNKS):
        here = slice(i * step, (i + 1) * step)
        value = tok[here].astype(F32) + (total.take(i) + obias[...])
        mid[here] = value
        unit, _ = unit_rows(value)
        full[here] = (unit * norm_gains[1:2] + norm_shifts[1:2]).astype(BF16)
        spread_mid.post(i)
        if i == 1:
            supply.tick(9)
    for i in range(CHUNKS):
        spread_mid.forward(i)
    for n in range(10, len(supply.items)):
        supply.tick(n)
    total.finish()
    spread_mid.finish()
    relay.finish(2)
    supply.ready(5)
    supply.finish()

    @pl.when(moved)
    def _():
        for i in range(CHUNKS):
            token(i).wait_send()
        for copy in packs():
            copy.wait_send()


def front(ids, tokens, numbers, tables, norm_gains, norm_shifts, obias, w3, wo, wu, cot):
    rows, width = tokens.shape
    n = 4 * rows
    cols = w3.shape[2]
    rank = tables[1].shape[1]
    packed = 4 * cols + 2 * wu.shape[1]
    items = 3 + (wo.shape[0] + wu.shape[0]) // 4 // ITEM + rows // ITEM
    low = lambda *s: jax.ShapeDtypeStruct(s, BF16)
    high = lambda *s: jax.ShapeDtypeStruct(s, F32)
    return pl.pallas_call(
        front_kernel,
        in_specs=[pl.BlockSpec(memory_space=pltpu.SMEM)] + [VMEM_SPEC] * 13 + [ANY_SPEC] * 4,
        out_specs=[VMEM_SPEC] * 12 + [ANY_SPEC] * 4,
        out_shape=[
            low(n, width), low(rows, width), low(rank, packed), high(*numbers.shape), low(4 * rank, width),
            low(n, 3 * cols), high(cols // HEAD_DIM, n), low(n, cols), low(n, rank), low(n, rank),
            low(n, width), high(rows, width), low(n, width), low(*w3.shape), low(*wo.shape), low(*wu.shape),
        ],
        scratch_shapes=[
            VM((rank, packed), BF16),
            VM((n, width), BF16), VM(w3.shape, BF16), VM(wo.shape, BF16), VM((n, rows), F32), VM((cols, n), BF16),
            VM((2 * rows, width), BF16), VM((rows, width), BF16), VM((rows, width), BF16),
        ]
        + sems(CHUNKS) + sems(2) + sems(items) + sems(items, 3) + sems(3, rows // ITEM)
        + sems(3, CHUNKS) + sems(2, 3, CHUNKS) + [pltpu.SemaphoreType.DMA((5,))],
        compiler_params=comm_params(1, 60),
        name="front",
    )(ids, tokens, numbers, *tables, norm_gains, norm_shifts, obias, w3, wo, wu, cot)


def mlp_kernel(
    nm, cot, wu, wu_role, wd, chosen, small, nums,
    part, gmid, tuo, tdi, tui, tdo, wd_role,
    wus, wds, hid, gg, stage, up_rank, g_down, down_rank, g_up,
    xs, xr, ss, sr, up_sem, down_sem, out_sem,
):
    at = places()
    moved = at["moved"]
    greet((at["core"], at["near"]), (at["cross"], at["left"], at["up"], at["both"]), moved)
    supply = Supply(at, [(wd, wd_role, True, ITEM)], xs, xr, ss, sr)

    @pl.when(moved)
    def _():
        supply.begin(1)

    n = nm.shape[0]
    rank = small.shape[0]
    count, tile = wus.shape[0], wus.shape[2]
    hidden = count * tile
    lines = tile // ITEM
    rows = n // 2
    au, bd = chosen[2 * rank : 3 * rank], chosen[3 * rank :]
    bu_at = small.shape[1] - 2 * hidden
    ad_at = small.shape[1] - hidden
    bias_at = nums.shape[1] - 128 - hidden
    size = hidden // lines

    def cut(i, q):
        return slice(q * size + i * ITEM, q * size + (i + 1) * ITEM)

    def columns(ref, first, i):
        return jnp.concatenate(
            [ref[:, first + q * size + i * ITEM : first + q * size + (i + 1) * ITEM] for q in range(lines)], axis=1
        )

    def load_up(i):
        for q in range(lines):
            span = pl.ds(q * size + i * ITEM, ITEM)
            fetch(wu.at[:, span], wu_role.at[:, span], wus.at[i, :, pl.ds(q * ITEM, ITEM)], up_sem.at[i, q])

    def await_up(i):
        for q in range(lines):
            span = pl.ds(q * size + i * ITEM, ITEM)
            pltpu.make_async_copy(wu.at[:, span], wus.at[i, :, pl.ds(q * ITEM, ITEM)], up_sem.at[i, q]).wait()

    def load_down(i):
        for q in range(lines):
            span = pl.ds(q * size + i * ITEM, ITEM)
            fetch(wd.at[span], wd_role.at[span], wds.at[i, pl.ds(q * ITEM, ITEM)], down_sem.at[i, q])

    def await_down(i):
        for q in range(lines):
            span = pl.ds(q * size + i * ITEM, ITEM)
            pltpu.make_async_copy(wd.at[span], wds.at[i, pl.ds(q * ITEM, ITEM)], down_sem.at[i, q]).wait()

    def by_rows(act):
        def body(r, carry):
            act(pl.ds(pl.multiple_of(r * rows, rows), rows))
            return carry

        lax.fori_loop(0, 2, body, 0)

    for i in range(count):
        load_up(i)
    up_rank[...] = dot_t(nm[...], au).astype(BF16)
    g_down[...] = dot_t(cot[...], bd).astype(BF16)
    for i in range(count):
        bu_i, bias_i = columns(small, bu_at, i), columns(nums, bias_at, i)
        await_up(i)

        def open_gate(here):
            gate = dot(nm[here], wus[i]) + dot(up_rank[here], bu_i) + bias_i
            value, slope = gelu_parts(gate)
            hid[i, here] = value.astype(BF16)
            gg[i, here] = slope.astype(BF16)

        by_rows(open_gate)
        supply.tick(i)
    for i in range(count):
        supply.ready_item(i)
        load_down(i)
        ad_i, bu_i = columns(small, ad_at, i), columns(small, bu_at, i)
        await_down(i)

        def close_gate(here):
            grad = dot_t(cot[here], wds[i]) + dot(g_down[here], ad_i)
            gg[i, here] = (grad * gg[i, here].astype(F32)).astype(BF16)

        by_rows(close_gate)
        up_part = dot_t(gg[i], bu_i)
        down_part = dot_t(hid[i], ad_i)
        if i == 0:
            g_up[...] = up_part
            down_rank[...] = down_part
        else:
            g_up[...] += up_part
            down_rank[...] += down_part
        one = t_dot(up_rank[...], gg[i])
        two = t_dot(g_down[...], hid[i])
        for q in range(lines):
            tuo[:, cut(i, q)] = one[:, q * ITEM : (q + 1) * ITEM]
            tdi[:, cut(i, q)] = two[:, q * ITEM : (q + 1) * ITEM]
    gu = g_up[...].astype(BF16)
    dr = down_rank[...].astype(BF16)
    up_rank[...] = gu
    g_down[...] = dr

    def store(slot, target, r):
        return pltpu.make_async_copy(stage.at[slot], target.at[pl.ds(r * rows, rows)], out_sem.at[slot])

    for r in range(2):
        here = slice(r * rows, (r + 1) * rows)
        value = dot(up_rank[here], au)
        for i in range(count):
            value = value + dot_t(gg[i, here], wus[i])
        if r > 0:
            store(0, gmid, r - 1).wait()
        stage[0] = value.astype(BF16)
        store(0, gmid, r).start()
        value = dot(g_down[here], bd)
        for i in range(count):
            value = value + dot(hid[i, here], wds[i])
        if r > 0:
            store(1, part, r - 1).wait()
        stage[1] = value.astype(BF16)
        store(1, part, r).start()
    tui[...] = t_dot(gu, nm[...])
    tdo[...] = t_dot(dr, cot[...])
    store(0, gmid, 1).wait()
    store(1, part, 1).wait()
    supply.finish()


def mlp(nm, cot, wu, wu_role, wd, chosen, small, nums):
    n, width = nm.shape
    hidden = wu.shape[1]
    rank = small.shape[0]
    items = wd.shape[0] // 4 // ITEM
    tile = hidden // items
    low = lambda *s: jax.ShapeDtypeStruct(s, BF16)
    high = lambda *s: jax.ShapeDtypeStruct(s, F32)
    return pl.pallas_call(
        mlp_kernel,
        in_specs=[VMEM_SPEC] * 2 + [ANY_SPEC] * 3 + [VMEM_SPEC] * 3,
        out_specs=[ANY_SPEC] * 2 + [VMEM_SPEC] * 4 + [ANY_SPEC],
        out_shape=[
            low(n, width), low(n, width), high(rank, hidden), high(rank, hidden), high(rank, width), high(rank, width),
            low(*wd.shape),
        ],
        scratch_shapes=[
            VM((items, width, tile), BF16), VM((items, tile, width), BF16), VM((items, n, tile), BF16),
            VM((items, n, tile), BF16), VM((2, n // 2, width), BF16),
            VM((n, rank), BF16), VM((n, rank), BF16), VM((n, rank), F32), VM((n, rank), F32),
        ]
        + sems(items) + sems(items, 3)
        + [pltpu.SemaphoreType.DMA((items, 4)), pltpu.SemaphoreType.DMA((items, 4)), pltpu.SemaphoreType.DMA((2,))],
        compiler_params=comm_params(3, 60),
        name="mlp",
    )(nm, cot, wu, wu_role, wd, chosen, small, nums)


class Tables:
    def __init__(self, at, pack, shared, home, gathered, every, buffers, semaphores):
        self.at, self.pack, self.shared, self.home = at, pack, shared, home
        self.gathered, self.every = gathered, every
        self.half_in, self.half, self.quarter_in = buffers
        (
            self.s1, self.r1, self.s2, self.r2, self.s3, self.r3, self.s4, self.r4, self.s5, self.r5, self.s6, self.r6,
            self.keep,
        ) = semaphores
        self.d, self.t = lax.axis_index("dp"), lax.axis_index("tensor")
        self.nd, self.nt = gathered.shape[0], every.shape[0]
        self.core, self.low = self.d % 2, self.t % 2
        self.wide = shared.shape[1] // 2
        self.narrow = self.wide // 2
        self.count = shared.shape[0]
        self.own = pack.shape[0] - self.count

    def first(self):
        away = pl.ds(pl.multiple_of((1 - self.core) * self.wide, self.wide), self.wide)
        return remote(self.shared.at[:, away], self.half_in, self.s1, self.r1, self.at["core"])

    def second(self):
        away = pl.ds(pl.multiple_of((1 - self.low) * self.narrow, self.narrow), self.narrow)
        return remote(self.half.at[:, away], self.quarter_in, self.s2, self.r2, self.at["near"])

    def third(self):
        return remote(self.pack, self.home, self.s3, self.r3, self.at["cross"])

    def fourth(self, k):
        peer = (lax.rem(self.d + k, self.nd), self.t)
        return remote(self.home, self.gathered.at[self.d], self.s4.at[k], self.r4.at[k], peer)

    def stay(self):
        return pltpu.make_async_copy(self.home, self.gathered.at[self.d], self.keep.at[0])

    def share_of(self, core):
        return pl.ds(core * (self.nd // 2), self.nd // 2)

    def fifth(self, k):
        peer = (self.d, lax.rem(self.t + k, self.nt))
        slots = self.share_of(self.core)
        mine = self.gathered.at[slots, pl.ds(self.own, self.count)]
        return remote(mine, self.every.at[self.t, slots], self.s5.at[k], self.r5.at[k], peer)

    def sixth(self, k):
        block = self.every.at[lax.rem(self.t + k, self.nt), self.share_of(self.core)]
        return remote(block, block, self.s6.at[k], self.r6.at[k], self.at["core"])

    def stay_every(self):
        mine = self.gathered.at[pl.ds(0, self.nd), pl.ds(self.own, self.count)]
        return pltpu.make_async_copy(mine, self.every.at[self.t], self.keep.at[1])

    def peers(self, act):
        def body(k, carry):
            act(self.fourth(k))
            return carry

        lax.fori_loop(1, self.nd, body, 0)

    def hop1(self):
        self.first().start()

    def hop2(self):
        self.first().wait_recv()
        mine = pl.ds(pl.multiple_of(self.core * self.wide, self.wide), self.wide)
        self.half[...] = (self.shared[:, mine].astype(F32) + self.half_in[...].astype(F32)).astype(BF16)
        self.second().start()

    def hop3(self):
        self.second().wait_recv()
        mine = pl.ds(pl.multiple_of(self.low * self.narrow, self.narrow), self.narrow)
        total = self.half[:, mine].astype(F32) + self.quarter_in[...].astype(F32)
        self.pack[self.own :] = total.astype(BF16)

        @pl.when(self.at["moved"])
        def _():
            self.third().start()

        @pl.when(jnp.logical_not(self.at["moved"]))
        def _():
            self.home[...] = self.pack[...]

    def hop4(self):
        @pl.when(self.at["moved"])
        def _():
            self.third().wait_recv()

        self.stay().start()
        self.peers(lambda copy: copy.start())

    def hop5(self):
        self.peers(lambda copy: copy.wait_recv())
        self.stay().wait()
        self.stay_every().start()
        for k in range(1, self.nt):
            self.fifth(k).start()

    def hop6(self):
        for k in range(1, self.nt):
            self.fifth(self.nt - k).wait_recv()
            self.sixth(k).start()

    def finish(self):
        self.first().wait_send()
        self.second().wait_send()

        @pl.when(self.at["moved"])
        def _():
            self.third().wait_send()

        self.peers(lambda copy: copy.wait_send())
        self.stay_every().wait()
        for k in range(1, self.nt):
            self.fifth(k).wait_send()
            self.sixth(k).wait()


def tables_scratch(nd, own, count, width):
    one = pltpu.SemaphoreType.DMA
    return (
        [
            VM((own + count, width // 4), BF16), VM((count, width), BF16), VM((own + count, width // 4), BF16),
            VM((count, width // 2), BF16), VM((count, width // 2), BF16), VM((count, width // 4), BF16),
        ],
        [one] * 6 + sems(nd) + sems(4) + sems(4) + [one((2,))],
    )


def back_kernel(
    gmid, mlp_part, x, w3, wqkv, wo, wo_role, cot, mid, tok, gains, dbias, proj, ctx, lse, rank_qkv, rank_out,
    small, chosen, nums, tuo, tdi, tui, tdo, ids,
    out, in_grad, own_early, every_early, own_late, every_late, all_ids,
    work, kept, gm, grad, gctx, gproj, dist, kt, gk, gv, wv, wov, side, far, mix, side2, far2, mix2, done, done2, low_rank,
    *rest,
):
    early_buffers, late_buffers = rest[:6], rest[6:12]
    early_sems, late_sems = rest[12:25], rest[25:38]
    rs, rr, ms, mr, ls, lr, gs, gr, os, orr, bs, br, ns, nr, load = rest[38:]
    at = places()
    moved = at["moved"]
    still = jnp.logical_not(moved)
    d, t = lax.axis_index("dp"), lax.axis_index("tensor")
    nd, nt = own_early.shape[0], every_early.shape[0]
    barrier = pltpu.get_barrier_semaphore()

    def hail(k, carry):
        pl.semaphore_signal(barrier, inc=1, device_id=(lax.rem(d + k, nd), t), device_id_type=MESH)
        return carry

    lax.fori_loop(1, nd, hail, 0)
    for k in range(1, nt):
        pl.semaphore_signal(barrier, inc=1, device_id=(d, lax.rem(t + k, nt)), device_id_type=MESH)

    @pl.when(moved)
    def _():
        pl.semaphore_signal(barrier, inc=1, device_id=at["cross"], device_id_type=MESH)

    pl.semaphore_wait(barrier, nd - 1 + nt - 1 + moved.astype(jnp.int32))

    rows = tok.shape[0]
    step = rows // CHUNKS
    cols = ctx.shape[1]
    rank = small.shape[0]
    heads = cols // HEAD_DIM
    scale = 1.0 / math.sqrt(HEAD_DIM)
    get_work = pltpu.make_async_copy(gmid, work, load.at[0])
    get_work.start()
    get_kept = [
        pltpu.make_async_copy(mlp_part.at[pl.ds(2 * j * rows, rows)], kept.at[pl.ds(j * rows, rows)], load.at[1 + j])
        for j in range(2)
    ]
    for copy in get_kept:
        copy.start()
    fetch(wo, wo_role, wov, load.at[3])
    all_ids[d] = ids[...]

    def number(k):
        return remote(ids, all_ids.at[d], ns.at[k], nr.at[k], (lax.rem(d + k, nd), t))

    def send_number(k, carry):
        number(k).start()
        return carry

    def await_number(k, carry):
        number(k).wait()
        return carry

    get_work.wait()
    total = Gathered(at, work, side, far, mix, rs, rr)
    spread = Spread(at, gm, gs, gr)
    total.begin()
    lax.fori_loop(1, nd, send_number, 0)
    for i in range(CHUNKS):
        here = slice(i * step, (i + 1) * step)
        unit, inverse = unit_rows(mid[here])
        value = cot[here].astype(F32) + unit_back(total.take(i), unit, inverse, gains[1:2])
        grad[here] = value
        gm[here] = value.astype(BF16)
        spread.post(i)
    pltpu.make_async_copy(wo, wov, load.at[3]).wait()
    bq, ao = small[:, : 3 * cols], small[:, 3 * cols : 4 * cols]
    aq, bo = chosen[0:rank], chosen[rank : 2 * rank]

    def context_rows(i, sums):
        here = pl.ds(i * rows, rows)
        g = gm[here]
        r = dot_t(g, bo).astype(BF16)
        gctx[here] = (dot_t(g, wov[...]) + dot(r, ao)).astype(BF16)
        return sums[0] + t_dot(rank_out[here], g), sums[1] + t_dot(r, ctx[here])

    sums = (jnp.zeros((rank, gm.shape[1]), F32), jnp.zeros((rank, cols), F32))
    sums = context_rows(0, sums)
    for i in range(2):
        spread.forward(i)
    spread.beside()
    sums = context_rows(1, sums)
    for i in range(2, CHUNKS):
        spread.forward(i)
    spread.finish()
    total.finish()
    for copy in get_kept:
        copy.wait()
    mlp = Gathered(at, mlp_part, side, far, mix, ms, mr, kept)
    mlp.send_away()
    mlp.send_home()
    sums = context_rows(2, sums)
    mlp.send_over()
    sums = context_rows(3, sums)
    pack, shared, home = early_buffers[:3]

    def lay(blocks, value):
        for k in range(value.shape[1] // cols):
            here = (blocks + k) * rank
            pack[here : here + rank] = value[:, k * cols : (k + 1) * cols].astype(BF16)

    lay(0, sums[1])
    lay(1, tuo)
    lay(1 + tuo.shape[1] // cols, tdi)
    shared[0:rank] = sums[0].astype(BF16)
    shared[rank : 2 * rank] = tui[...].astype(BF16)
    shared[2 * rank :] = tdo[...].astype(BF16)
    early = Tables(at, pack, shared, home, own_early, every_early, early_buffers[3:], early_sems)
    early.hop1()
    get_x = pltpu.make_async_copy(x, gm, load.at[4])
    get_x.start()
    for j in range(3):
        fetch(w3.at[j], wqkv.at[j], wv.at[j], load.at[5 + j])

    me = 2 * (d % 2) + t % 2
    base = nums.shape[1] - 128
    slopes = head_slopes(me, heads)
    kt[...] = proj[:, cols : 2 * cols].T
    gk[...] = jnp.zeros_like(gk)
    gv[...] = jnp.zeros_like(gv)

    def attend_step(i, carry):
        here = pl.ds(pl.multiple_of(i * rows, rows), rows)
        distances(me, nums[0:1, base : base + 1], nums[0:1, base + 1 : base + 2], rows, i, dist)
        for h in range(heads):
            span = slice(h * HEAD_DIM, (h + 1) * HEAD_DIM)
            q, g = proj[here, span], gctx[here, span]
            keys = proj[:, cols + h * HEAD_DIM : cols + (h + 1) * HEAD_DIM]
            values = proj[:, 2 * cols + h * HEAD_DIM : 2 * cols + (h + 1) * HEAD_DIM]
            s = dot_t(keys, q) * (scale * LOG2E) - dist[...] * slopes[h]
            p = jnp.exp2(s - lse[h : h + 1, here])
            gv[:, span] += dot(p.astype(BF16), g)
            gp = dot_t(values, g)
            inner = jnp.sum(p * gp, axis=0, keepdims=True)
            gsc = (p * (gp - inner)).astype(BF16)
            gk[:, span] += dot(gsc, q)
            gproj[here, span] = (dot(kt[span, :], gsc).T * scale).astype(BF16)
        return carry

    lax.fori_loop(0, 2, attend_step, 0)
    early.hop2()
    lax.fori_loop(2, 4, attend_step, 0)
    early.hop3()
    gproj[:, cols : 2 * cols] = (gk[...] * scale).astype(BF16)
    gproj[:, 2 * cols :] = gv[...].astype(BF16)

    def out_back(i):
        here = pl.ds(i * step, step)
        return remote(done.at[here], out.at[here], os.at[i], orr.at[i], at["cross"])

    def grad_back(i):
        here = pl.ds(i * step, step)
        return remote(done2.at[here], in_grad.at[here], bs.at[i], br.at[i], at["cross"])

    for i in range(CHUNKS):
        here = slice(i * step, (i + 1) * step)
        value = (mid[here] + (mlp.take(i) + dbias[...])).astype(BF16)

        @pl.when(moved)
        def _():
            done[here] = value
            out_back(i).start()

        @pl.when(still)
        def _():
            out[here] = value

    get_x.wait()
    for j in range(3):
        pltpu.make_async_copy(w3.at[j], wv.at[j], load.at[5 + j]).wait()
    pack, shared, home = late_buffers[:3]
    low = dot_t(gproj[...], bq).astype(BF16)
    lay_rows = t_dot(rank_qkv[...], gproj[...]).astype(BF16)
    for j in range(3):
        pack[j * rank : (j + 1) * rank] = lay_rows[:, j * cols : (j + 1) * cols]
    shared[...] = t_dot(low, gm[...]).astype(BF16)
    low_rank[...] = low
    late = Tables(at, pack, shared, home, own_late, every_late, late_buffers[3:], late_sems)
    late.hop1()

    def input_rows(i):
        here = pl.ds(i * rows, rows)
        acc = dot(low_rank[here], aq)
        for j in range(3):
            acc = acc + dot_t(gproj[here, j * cols : (j + 1) * cols], wv[j])
        work[here] = acc.astype(BF16)

    last = Gathered(at, work, side2, far2, mix2, ls, lr)
    input_rows(3)
    last.send_away()
    early.hop4()
    input_rows(1)
    last.send_home()
    late.hop2()
    input_rows(2)
    last.send_over()
    late.hop3()
    input_rows(0)
    for i in range(CHUNKS):
        here = slice(i * step, (i + 1) * step)
        unit, inverse = unit_rows(tok[here].astype(F32))
        value = (grad[here] + unit_back(last.take(i), unit, inverse, gains[0:1])).astype(BF16)

        @pl.when(moved)
        def _():
            done2[here] = value
            grad_back(i).start()

        @pl.when(still)
        def _():
            in_grad[here] = value

        if i == 0:
            late.hop4()
        if i == 1:
            early.hop5()
        if i == 3:
            late.hop5()
    early.hop6()
    late.hop6()
    lax.fori_loop(1, nd, await_number, 0)
    mlp.finish()
    last.finish()
    early.finish()
    late.finish()

    @pl.when(moved)
    def _():
        for i in range(CHUNKS):
            out_back(i).wait()
            grad_back(i).wait()


def back(nd, nt, gmid, mlp_part, x, w3, wqkv, wo, wo_role, cot, mid, tok, gains, dbias, proj, ctx, lse, rank_qkv,
         rank_out, small, chosen, nums, tuo, tdi, tui, tdo, ids):
    rows, width = tok.shape
    n = 4 * rows
    cols = ctx.shape[1]
    rank = small.shape[0]
    early_own = (1 + 2 * tuo.shape[1] // cols) * rank
    low = lambda *s: jax.ShapeDtypeStruct(s, BF16)
    early = tables_scratch(nd, early_own, 3 * rank, width)
    late = tables_scratch(nd, 3 * rank, rank, width)
    return pl.pallas_call(
        back_kernel,
        in_specs=[ANY_SPEC] * 7 + [VMEM_SPEC] * 18,
        out_specs=[VMEM_SPEC] * 2 + [ANY_SPEC] * 4 + [VMEM_SPEC],
        out_shape=[
            low(rows, width), low(rows, width),
            low(nd, early_own + 3 * rank, width // 4), low(nt, nd, 3 * rank, width // 4),
            low(nd, 4 * rank, width // 4), low(nt, nd, rank, width // 4),
            jax.ShapeDtypeStruct((nd,) + ids.shape, jnp.int32),
        ],
        scratch_shapes=[
            VM((n, width), BF16), VM((2 * rows, width), BF16), VM((n, width), BF16), VM((rows, width), F32),
            VM((n, cols), BF16), VM((n, 3 * cols), BF16), VM((n, rows), F32), VM((cols, n), BF16),
            VM((n, cols), F32), VM((n, cols), F32), VM(w3.shape, BF16), VM(wo.shape, BF16),
            VM((2 * rows, width), BF16), VM((rows, width), BF16), VM((rows, width), BF16),
            VM((2 * rows, width), BF16), VM((rows, width), BF16), VM((rows, width), BF16),
            VM((rows, width), BF16), VM((rows, width), BF16), VM((n, rank), BF16),
        ]
        + early[0] + late[0] + early[1] + late[1]
        + sems(3, CHUNKS) * 4 + sems(CHUNKS) * 2 + sems(nd) + [pltpu.SemaphoreType.DMA((8,))],
        compiler_params=comm_params(2, 62),
        name="back",
    )(gmid, mlp_part, x, w3, wqkv, wo, wo_role, cot, mid, tok, gains, dbias, proj, ctx, lse, rank_qkv, rank_out,
      small, chosen, nums, tuo, tdi, tui, tdo, ids)


def combine_kernel(ids, own_early, every_early, own_late, every_late, gqi, gqo, goi, goo, gui, guo, gdi, gdo):
    nd = own_early.shape[0]
    cols = goi.shape[2]
    wide = guo.shape[2]
    rank = goi.shape[1]
    quarter = every_late.shape[3]
    for ref in (gqi, gqo, goi, goo, gui, guo, gdi, gdo):
        ref[...] = jnp.zeros_like(ref)

    def block(ref, s, k):
        return ref[s, k * rank : (k + 1) * rank].astype(F32)

    def add(s, carry):
        e = [ids[s, 0, k] for k in range(4)]
        many = wide // cols
        for j in range(3):
            gqo[e[0], j] += block(own_late, s, j)
        goi[e[1]] += block(own_early, s, 0)
        for j in range(many):
            at = slice(j * cols, (j + 1) * cols)
            guo[e[2], :, at] += block(own_early, s, 1 + j)
            gdi[e[3], :, at] += block(own_early, s, 1 + many + j)
        for z in range(every_late.shape[0]):
            at = slice(z * quarter, (z + 1) * quarter)
            gqi[e[0], :, at] += every_late[z, s].astype(F32)
            goo[e[1], :, at] += every_early[z, s, 0:rank].astype(F32)
            gui[e[2], :, at] += every_early[z, s, rank : 2 * rank].astype(F32)
            gdo[e[3], :, at] += every_early[z, s, 2 * rank :].astype(F32)
        return carry

    lax.fori_loop(0, nd, add, 0)


def combine(ids, own_early, every_early, own_late, every_late, tables, cols, wide):
    rank = every_late.shape[2]
    width = every_late.shape[0] * every_late.shape[3]
    high = lambda *s: jax.ShapeDtypeStruct(s, F32)
    full = high(tables, rank, width)
    return pl.pallas_call(
        combine_kernel,
        in_specs=[pl.BlockSpec(memory_space=pltpu.SMEM)] + [VMEM_SPEC] * 4,
        out_specs=[VMEM_SPEC] * 8,
        out_shape=[
            full, high(tables, 3, rank, cols), high(tables, rank, cols), full, full, high(tables, rank, wide),
            high(tables, rank, wide), full,
        ],
        compiler_params=params(48),
        name="combine",
    )(ids, own_early, every_early, own_late, every_late)


def body(
    tokens, cotangent, norm_gains, norm_shifts, query_key_value_weight, b_qv, output_weight,
    output_bias_vector, up_weight, b_up, down_weight, down_bias_vector, adapter_query_key_value_input,
    qkv_out, adapter_output_input, adapter_output_output, adapter_up_input, up_out, down_in,
    adapter_down_output, offsets, adapter_ids,
):
    nd, nt = lax.axis_size("dp"), lax.axis_size("tensor")
    rows, width = tokens.shape
    local = output_weight.shape[0]
    hidden_width = up_weight.shape[1]
    tables = adapter_up_input.shape[0]

    w3 = jnp.transpose(query_key_value_weight, (1, 0, 2))
    b3 = jnp.transpose(qkv_out, (0, 2, 1, 3))
    extra = jnp.pad(jnp.concatenate([offsets, adapter_ids], 1).astype(F32), ((0, 0), (0, 122)))
    numbers = jnp.concatenate([b_qv.reshape(1, 2 * local), b_up.reshape(1, hidden_width), extra], 1)
    tables_in = (
        b3, adapter_output_input, up_out, down_in, adapter_query_key_value_input, adapter_output_output,
        adapter_up_input, adapter_down_output,
    )
    (
        x, tok, small, nums, chosen, proj, lse, ctx, rank_qkv, rank_out, nm, middle, cot, wqkv, wo, wu,
    ) = front(
        adapter_ids[0], tokens, numbers, tables_in, norm_gains, norm_shifts, output_bias_vector.reshape(1, width),
        w3, output_weight, up_weight, cotangent,
    )
    part, gmid, t_up_out, t_down_in, t_up_in, t_down_out, _ = mlp(
        nm, cot, up_weight, wu, down_weight, chosen, small, nums
    )
    result, in_grad, own_early, every_early, own_late, every_late, everyone = back(
        nd, nt, gmid, part, x, w3, wqkv, output_weight, wo, cot[:rows], middle, tok, norm_gains,
        down_bias_vector.reshape(1, width), proj, ctx, lse, rank_qkv, rank_out, small, chosen, nums,
        t_up_out, t_down_in, t_up_in, t_down_out, jnp.pad(adapter_ids, ((0, 0), (0, 124))),
    )
    gqi, gqo, goi, goo, gui, guo, gdi, gdo = combine(
        everyone, own_early, every_early, own_late, every_late, tables, local, hidden_width
    )
    return (result, in_grad, gqi, jnp.transpose(gqo, (0, 2, 1, 3)), goi, goo, gui, guo, gdi, gdo)


def solution(mesh):
    placed = (
        P(("dp", "tensor"), None), P(("dp", "tensor"), None), P(), P(), P(None, None, "tensor"), P(None, "tensor"),
        P("tensor", None), P(), P(None, "tensor"), P("tensor"), P("tensor", None), P(), P(),
        P(None, None, None, "tensor"), P(None, None, "tensor"), P(), P(), P(None, None, "tensor"),
        P(None, None, "tensor"), P(), P("dp", None), P("dp", None),
    )
    return jax.shard_map(
        body, mesh=mesh, in_specs=placed,
        out_specs=(
            P(("dp", "tensor"), None), P(("dp", "tensor"), None), P(), P(None, None, None, "tensor"),
            P(None, None, "tensor"), P(), P(), P(None, None, "tensor"), P(None, None, "tensor"), P(),
        ),
        check_vma=False,
    )
```
